512 devices in a mesh: gx: 16 (over y_lo, x), gy: 16 (over z, y_hi), col: 2 (over core).
Axes of the slice: x: 4, y: 8 (y_hi: 2, y_lo: 4; y = y_hi * 4 + y_lo), z: 8, core: 2. Of those that a mesh axis runs over, the one named last changes fastest.
Arguments:
- density: float32 [10, 10, 10, 64, 2048], P('col', None, None, 'gx', 'gy'), may hold values from -6 to 6
- velocity: float32 [2, 64, 2048], P(None, 'gx', 'gy'), may hold values from -3 to 3
- shear_rates: float32 [4, 64, 2048], P(None, 'gx', 'gy'), may hold values from -4 to 4
- hermite_matrix: float32 [10, 10], replicated, may hold values from -2 to 2
- laguerre_matrix: float32 [10, 10], replicated, may hold values from -2 to 2
- flow_first: float32 [4, 10, 10], replicated, may hold values from -2 to 2
- flow_second: float32 [4, 10, 10], replicated, may hold values from -2 to 2
- stress_weights: float32 [3, 10, 10, 10], P(None, 'col'), may hold values from -0.1875 to 0.1875
Outputs:
- advanced: float32 [10, 10, 10, 64, 2048], P('col', None, None, 'gx', 'gy')
- stress: float32 [3, 64, 2048], P(None, 'gx', 'gy')
The draws below stay inside these ranges and needn't reach their ends.
All inputs are finite; a program needn't handle non-finite values.
Results may differ from the reference program's by a relative error of at most 0.0003.
Values sent between devices are 32-bit elements; how exact they have to be, the bound alone decides.
No kernel may reach another device: no remote copies, remote signals or barrier semaphores. Data moves between devices by JAX's collectives and lax.ppermute only.
A program may use at most 128 MiB of HBM per device.

```python
import jax
import jax.numpy as jnp
from jax import lax

HM = 10
LM = 10
NX = 64
NY = 2048


def levels(stream_key, shape, shards, least, top_value):
    def one(position, parts):
        draws = jax.random.uniform(jax.random.fold_in(jax.random.fold_in(stream_key, 6), position), (parts,), jnp.float32, least / len(shards), top_value / len(shards))
        return jnp.repeat(jnp.exp(draws), shape[position] // parts).reshape((-1,) + (1,) * (len(shape) - position - 1))

    level = one(*shards[0])
    for cut in shards[1:]:
        level = level * one(*cut)
    return level


def gaussian(rng, dims, scale, most, shards=(), kind=jnp.bfloat16):
    entries = scale * jax.random.normal(rng, dims, jnp.float32)
    if shards:
        entries = entries * levels(rng, dims, shards, -0.22, 0.18)
    return jnp.clip(entries, -most, most).astype(kind)


def setup_inputs(seed: int = 0) -> dict:
    streams_of = jax.random.split(jax.random.key(seed), 9)
    return {
        "density": gaussian(streams_of[0], (HM, HM, LM, NX, NY), 1.0, 6.0, ((0, 2), (3, 16), (4, 16)), jnp.float32),
        "velocity": gaussian(streams_of[1], (2, NX, NY), 1.0, 3.0, ((1, 16), (2, 16)), jnp.float32),
        "shear_rates": gaussian(streams_of[2], (4, NX, NY), 1.0, 4.0, ((1, 16), (2, 16)), jnp.float32),
        "hermite_matrix": gaussian(streams_of[3], (HM, HM), HM ** -0.5, 2.0, (), jnp.float32),
        "laguerre_matrix": gaussian(streams_of[4], (LM, LM), LM ** -0.5, 2.0, (), jnp.float32),
        "flow_first": gaussian(streams_of[5], (4, HM, HM), HM ** -0.5, 2.0, (), jnp.float32),
        "flow_second": gaussian(streams_of[6], (4, HM, HM), HM ** -0.5, 2.0, (), jnp.float32),
        "stress_weights": gaussian(streams_of[7], (3, HM, HM, LM), (HM * HM * LM) ** -0.5, 0.1875, ((1, 2),), jnp.float32),
    }


time_step = 0.1
highest = lax.Precision.HIGHEST


def stencil(minus_two, minus_one, center, plus_one, plus_two, speed):
    back = 1.5 * center - 2.0 * minus_one + 0.5 * minus_two
    front = -1.5 * center + 2.0 * plus_one - 0.5 * plus_two
    return speed * jnp.where(speed > 0, back, front)


def config_rate(center, gradient, hermite_matrix, laguerre_matrix, flow_first, flow_second):
    rate = jnp.einsum('ap,pqr...->aqr...', hermite_matrix, center, precision=highest)
    rate = rate + jnp.einsum('bq,pqr...->pbr...', hermite_matrix, center, precision=highest)
    rate = rate + jnp.einsum('cr,pqr...->pqc...', laguerre_matrix, center, precision=highest)
    for component in range(4):
        inner = jnp.einsum('bq,pqr...->pbr...', flow_second[component], center, precision=highest)
        outer = jnp.einsum('ap,pqr...->aqr...', flow_first[component], inner, precision=highest)
        rate = rate + gradient[component] * outer
    return rate


def reference(density, velocity, shear_rates, hermite_matrix, laguerre_matrix, flow_first, flow_second, stress_weights):
    offsets = jnp.arange(-2, 3, dtype=jnp.int32)
    positions = jnp.arange(NX, dtype=jnp.int32)

    def one_row(x_index):
        picked = ((x_index + offsets) % NX).astype(jnp.int32)
        rows = jnp.take(density, picked, axis=3)
        center = rows[:, :, :, 2, :]
        stream_speed = velocity[0, x_index]
        normal_speed = velocity[1, x_index]
        across = stencil(rows[:, :, :, 0, :], rows[:, :, :, 1, :], center, rows[:, :, :, 3, :], rows[:, :, :, 4, :], stream_speed)
        padded = jnp.pad(center, ((0, 0), (0, 0), (0, 0), (2, 2)))
        normal = stencil(padded[..., 0:NY], padded[..., 1:NY + 1], center, padded[..., 3:NY + 3], padded[..., 4:NY + 4], normal_speed)
        transport = across + normal
        gradient = shear_rates[:, x_index]
        rate = config_rate(center, gradient, hermite_matrix, laguerre_matrix, flow_first, flow_second)
        advanced_row = center + time_step * (rate - transport)
        stress_row = jnp.einsum('spqr,pqry->sy', stress_weights, advanced_row, precision=highest)
        return advanced_row, stress_row

    advanced_rows, stress_rows = lax.map(one_row, positions)
    advanced = jnp.moveaxis(advanced_rows, 0, 3)
    stress = jnp.moveaxis(stress_rows, 0, 1)
    return advanced, stress
```

```python
import functools

import jax
import jax.numpy as jnp
from jax import lax
from jax.experimental import pallas as pl
from jax.experimental.pallas import tpu as pltpu
from jax.sharding import PartitionSpec as P

time_step = 0.1
highest = lax.Precision.HIGHEST
f32 = jnp.float32
bf16 = jnp.bfloat16

ROWS = 2000
PQ = 50
RX = 40
PQ_PAD = 56
K_HALF = 64
N_PAIR = 20
MODES_P = 100
MODES_PAD = 104


def upwind(speed):
    plus = jnp.maximum(speed, 0.0)
    minus = jnp.minimum(speed, 0.0)
    t = time_step
    center = (-1.5 * t) * jnp.abs(speed)
    return center, (2 * t) * plus, (-0.5 * t) * plus, (-2 * t) * minus, (0.5 * t) * minus


def tens(value):
    total = jnp.zeros_like(value)
    for j in range(1, 5):
        total = total + (value >= 10 * j).astype(jnp.int32)
    return total


def iota(shape, dim):
    return lax.broadcasted_iota(jnp.int32, shape, dim)


def one_hot(condition):
    return jnp.where(condition, 1.0, 0.0).astype(f32)


def halo_kernel(x_ref, low_ref, high_ref):
    for k in range(2):
        low_ref[0, k, 0:MODES_P, :] = x_ref[pl.ds(k, MODES_P, stride=4), :]
        high_ref[0, k, 0:MODES_P, :] = x_ref[pl.ds(2 + k, MODES_P, stride=4), :]


def x_halos(rows):
    shape = jax.ShapeDtypeStruct((5, 2, MODES_PAD, 128), f32)
    spec = pl.BlockSpec((1, 2, MODES_PAD, 128), lambda p: (p, 0, 0, 0))
    return pl.pallas_call(
        halo_kernel,
        grid=(5,),
        in_specs=[pl.BlockSpec((400, 128), lambda p: (p, 0))],
        out_specs=[spec, spec],
        out_shape=[shape, shape],
        cost_estimate=pl.CostEstimate(flops=0, bytes_accessed=2 * ROWS * 512, transcendentals=0),
        name="x_halos",
    )(rows)


def edge_kernel(x_ref, low_ref, high_ref, rows_ref):
    rows_ref[96:128, :] = jnp.zeros((32, 128), f32)
    lane = iota((8, 128), 1)
    row = iota((8, 128), 0)
    pick = one_hot(((row < 2) & (lane == row)) | ((row >= 2) & (row < 4) & (lane == row + 124)))
    for x in range(4):
        rows_ref[0:MODES_P, :] = x_ref[pl.ds(x, MODES_P, stride=4), :]
        edges = lax.dot_general(
            pick, rows_ref[...], (((1,), (1,)), ((), ())), precision=highest, preferred_element_type=f32
        )
        low_ref[:, x * 128 : (x + 1) * 128] = edges[0:2]
        high_ref[:, x * 128 : (x + 1) * 128] = edges[2:4]


def y_edges(rows):
    shape = jax.ShapeDtypeStruct((2, 5 * 512), f32)
    spec = pl.BlockSpec((2, 512), lambda p: (0, p))
    return pl.pallas_call(
        edge_kernel,
        grid=(5,),
        in_specs=[pl.BlockSpec((400, 128), lambda p: (p, 0))],
        out_specs=[spec, spec],
        out_shape=[shape, shape],
        scratch_shapes=[pltpu.VMEM((128, 128), f32)],
        cost_estimate=pl.CostEstimate(flops=0, bytes_accessed=ROWS * 512, transcendentals=0),
        name="y_edges",
    )(rows)


def split(value):
    high = value.astype(bf16)
    low = (value - high.astype(f32)).astype(bf16)
    return high, low


def coupling(start, first, second, hermite):
    rows = 5 * PQ_PAD

    def row_ids(width):
        i = iota((rows, width), 0)
        c = jnp.zeros_like(i)
        for j in range(1, 5):
            c = c + (i >= PQ_PAD * j).astype(jnp.int32)
        ab = i - PQ_PAD * c
        a = tens(ab)
        return c, a + start, ab - 10 * a, ab < PQ

    def expand(table, index, c, valid):
        t40 = iota((rows, 40), 1)
        t10 = iota((rows, 10), 1)
        c40, a40, b40, ok40 = row_ids(40)
        c10, a10, b10, ok10 = row_ids(10)
        i40 = a40 if index == 0 else b40
        i10 = a10 if index == 0 else b10
        pick_flow = one_hot(ok40 & (c40 < 4) & (t40 == 4 * i40 + c40))
        pick_spring = one_hot(ok10 & (c10 == 4) & (t10 == i10))
        return jnp.dot(pick_flow, table, precision=highest, preferred_element_type=f32) + jnp.dot(
            pick_spring, hermite, precision=highest, preferred_element_type=f32
        )

    def columns(height):
        k = iota((height, 128), 1)
        other = k >= K_HALF
        kk = jnp.where(other, k - K_HALF, k)
        p_here = tens(kk)
        p = p_here + jnp.where(other, 5 - start, start)
        return p, kk - 10 * p_here, kk < PQ

    c, a, b, valid = row_ids(128)
    p10, q10, ok10 = columns(10)
    source = iota((10, 128), 0)
    left = expand(first, 0, c, valid)
    right = expand(second, 1, c, valid)
    left = jnp.dot(left, one_hot(ok10 & (source == p10)), precision=highest, preferred_element_type=f32)
    right = jnp.dot(right, one_hot(ok10 & (source == q10)), precision=highest, preferred_element_type=f32)
    p, q, ok = columns(rows)
    spring = c == 4
    both = left * jnp.where(spring, one_hot(b == q), right)
    both = both + jnp.where(spring & (a == p), right, 0.0)
    return time_step * both


def main_kernel(
    place_ref,
    laguerre_ref,
    own_hbm,
    other_hbm,
    velocity_ref,
    shear_ref,
    first_ref,
    second_ref,
    hermite_ref,
    out_hbm,
    own_ref,
    other_ref,
    turned_ref,
    rate_ref,
    result_ref,
    wide_ref,
    narrow_ref,
    coef_ref,
    sems,
):
    copy_own = pltpu.make_async_copy(own_hbm, own_ref.at[0:ROWS], sems.at[0])
    copy_other = pltpu.make_async_copy(other_hbm, other_ref.at[0:ROWS], sems.at[1])
    copy_own.start()
    copy_other.start()
    zeros = jnp.zeros((K_HALF * RX - ROWS, 128), f32)
    own_ref[ROWS:, :] = zeros
    other_ref[ROWS:, :] = zeros

    matrix = coupling(place_ref[0], first_ref[...], second_ref[...], hermite_ref[...])
    matrix_high, matrix_low = split(matrix)
    wide_ref[:, 0:128] = matrix_high
    wide_ref[:, 128:256] = matrix_high
    narrow_ref[...] = matrix_low

    u = velocity_ref[0:4, :]
    v = velocity_ref[4:8, :]
    lane = iota((4, 128), 1)
    u0, um1, um2, up1, up2 = upwind(u)
    v0, vm1, vm2, vp1, vp2 = upwind(v)
    coefs = (
        1.0 + u0 + v0,
        um1,
        um2,
        up1,
        up2,
        jnp.where(lane >= 1, vm1, 0.0),
        jnp.where(lane >= 2, vm2, 0.0),
        jnp.where(lane < 127, vp1, 0.0),
        jnp.where(lane < 126, vp2, 0.0),
    )
    for i, c in enumerate(coefs):
        coef_ref[i, 0:4, :] = c

    copy_own.wait()
    copy_other.wait()

    def pair(i, carry):
        parts = []
        for t in range(2):
            rx = 2 * i + t
            own = own_ref[pl.ds(rx, K_HALF, stride=RX), :]
            other = other_ref[pl.ds(rx, K_HALF, stride=RX), :]
            turned_ref[pl.ds(pl.multiple_of(rx * K_HALF, K_HALF), K_HALF), :] = own
            own_high, own_low = split(own)
            other_high, other_low = split(other)
            parts.append(jnp.concatenate([own_high, other_high, own_low, other_low], axis=0))
        data = jnp.concatenate(parts, axis=1)
        product = jnp.dot(wide_ref[...], data, preferred_element_type=f32)
        product = product + jnp.dot(narrow_ref[...], data[0:128], preferred_element_type=f32)
        for t in range(2):
            rx = 2 * i + t
            x = lax.rem(rx, 4)
            part = product[:, t * 128 : (t + 1) * 128]
            total = part[4 * PQ_PAD : 5 * PQ_PAD]
            for c in range(4):
                total = total + shear_ref[pl.ds(4 * c + x, 1), :] * part[c * PQ_PAD : (c + 1) * PQ_PAD]
            rate_ref[pl.ds(pl.multiple_of(rx * PQ_PAD, PQ_PAD), PQ_PAD), :] = total
        return carry

    lax.fori_loop(0, N_PAIR, pair, 0)

    def strip(j, carry):
        def field(r, x):
            return turned_ref[pl.ds(pl.multiple_of((4 * r + x) * K_HALF + 8 * j, 8), 8), :]

        for x in range(4):
            def coef(i):
                return coef_ref[i, x : x + 1, :]

            here = [field(r, x) for r in range(10)]
            for r in range(10):
                mixed = laguerre_ref[r, 0] * here[0]
                for s in range(1, 10):
                    mixed = mixed + laguerre_ref[r, s] * here[s]
                f = here[r]
                total = rate_ref[pl.ds(pl.multiple_of((4 * r + x) * PQ_PAD + 8 * j, 8), 8), :]
                total = total + time_step * mixed + coef(0) * f
                for shift, i in ((-1, 1), (-2, 2), (1, 3), (2, 4)):
                    if 0 <= x + shift < 4:
                        total = total + coef(i) * field(r, x + shift)
                for shift, i in ((1, 5), (2, 6), (127, 7), (126, 8)):
                    total = total + coef(i) * pltpu.roll(f, shift, 1)
                result_ref[pl.ds(j * (8 * RX) + 4 * r + x, 8, stride=RX), :] = total
        return carry

    lax.fori_loop(0, PQ_PAD // 8, strip, 0)
    copy_out = pltpu.make_async_copy(result_ref.at[0:ROWS], out_hbm, sems.at[2])
    copy_out.start()
    copy_out.wait()


def main(place, laguerre, own, other, velocity, shear, first, second, hermite):
    vmem = pl.BlockSpec(memory_space=pltpu.VMEM)
    smem = pl.BlockSpec(memory_space=pltpu.SMEM)
    hbm = pl.BlockSpec(memory_space=pl.ANY)
    return pl.pallas_call(
        main_kernel,
        in_specs=[smem, smem, hbm, hbm, vmem, vmem, vmem, vmem, vmem],
        out_specs=hbm,
        out_shape=jax.ShapeDtypeStruct((ROWS, 128), f32),
        scratch_shapes=[
            pltpu.VMEM((K_HALF * RX, 128), f32),
            pltpu.VMEM((K_HALF * RX, 128), f32),
            pltpu.VMEM((K_HALF * RX, 128), f32),
            pltpu.VMEM((PQ_PAD * RX, 128), f32),
            pltpu.VMEM((PQ_PAD * RX, 128), f32),
            pltpu.VMEM((5 * PQ_PAD, 256), bf16),
            pltpu.VMEM((5 * PQ_PAD, 128), bf16),
            pltpu.VMEM((9, 8, 128), f32),
            pltpu.SemaphoreType.DMA((3,)),
        ],
        compiler_params=pltpu.CompilerParams(vmem_limit_bytes=24 << 20),
        cost_estimate=pl.CostEstimate(flops=2 * 280 * 384 * 5120, bytes_accessed=3 * ROWS * 512, transcendentals=0),
        name="main_step",
    )(place, laguerre, own, other, velocity, shear, first, second, hermite)


def final_kernel(
    partial_ref, left_ref, right_ref, below_ref, above_ref, velocity_ref, weight_ref, out_ref, stress_ref
):
    p = pl.program_id(0)
    u = velocity_ref[0:4, :]
    v = velocity_ref[4:8, :]
    lane4 = iota((4, 128), 1)
    _, um1, um2, up1, up2 = upwind(u)
    _, vm1, vm2, vp1, vp2 = upwind(v)
    near = jnp.where(lane4 == 0, vm1, jnp.where(lane4 == 127, vp1, 0.0))
    far = jnp.where(lane4 <= 1, vm2, jnp.where(lane4 >= 126, vp2, 0.0))

    edges = jnp.concatenate([below_ref[...], above_ref[...], jnp.zeros((4, 512), f32)], axis=0)
    high = edges.astype(bf16).astype(f32)
    rest = edges - high
    middle = rest.astype(bf16).astype(f32)
    low = rest - middle
    stacked = jnp.concatenate([high, middle, low, jnp.zeros((8, 512), f32)], axis=0).astype(bf16)
    row = lax.rem(iota((32, 256), 0), 8)
    lane = iota((32, 256), 1)
    hit = (row == 1) & ((lane == 0) | (lane == 129))
    hit = hit | ((row == 2) & ((lane == 127) | (lane == 254)))
    hit = hit | ((row == 0) & (lane == 128))
    hit = hit | ((row == 3) & (lane == 255))
    spread = lax.dot_general(
        stacked, one_hot(hit).astype(bf16), (((0,), (0,)), ((), ())), preferred_element_type=f32
    )

    @pl.when(p == 0)
    def _():
        stress_ref[...] = jnp.zeros_like(stress_ref)

    left_far = left_ref[0, 0, 0:MODES_P, :]
    left_near = left_ref[0, 1, 0:MODES_P, :]
    right_near = right_ref[0, 0, 0:MODES_P, :]
    right_far = right_ref[0, 1, 0:MODES_P, :]
    for x in range(4):
        total = partial_ref[pl.ds(x, MODES_P, stride=4), :]
        total = total + near[x : x + 1] * spread[x * 128 : x * 128 + MODES_P, 0:128]
        total = total + far[x : x + 1] * spread[x * 128 : x * 128 + MODES_P, 128:256]
        if x == 0:
            total = total + um1[0:1] * left_near + um2[0:1] * left_far
        if x == 1:
            total = total + um2[1:2] * left_near
        if x == 2:
            total = total + up2[2:3] * right_near
        if x == 3:
            total = total + up1[3:4] * right_near + up2[3:4] * right_far
        out_ref[pl.ds(x, MODES_P, stride=4), :] = total
        for s in range(3):
            moment = jnp.sum(weight_ref[0, :, s : s + 1] * total, axis=0, keepdims=True)
            stress_ref[4 * s + x : 4 * s + x + 1, :] += moment


def final(partial, left, right, below, above, velocity, weights):
    halo = pl.BlockSpec((1, 2, MODES_PAD, 128), lambda p: (p, 0, 0, 0))
    edge = pl.BlockSpec((2, 512), lambda p: (0, p))
    rows = pl.BlockSpec((400, 128), lambda p: (p, 0))
    return pl.pallas_call(
        final_kernel,
        grid=(5,),
        in_specs=[
            rows,
            halo,
            halo,
            edge,
            edge,
            pl.BlockSpec((8, 128), lambda p: (0, 0)),
            pl.BlockSpec((1, MODES_P, 3), lambda p: (p, 0, 0)),
        ],
        out_specs=[rows, pl.BlockSpec((12, 128), lambda p: (0, 0))],
        out_shape=[jax.ShapeDtypeStruct((ROWS, 128), f32), jax.ShapeDtypeStruct((12, 128), f32)],
        cost_estimate=pl.CostEstimate(flops=20 * ROWS * 128, bytes_accessed=4 * ROWS * 512, transcendentals=0),
        name="final_step",
    )(partial, left, right, below, above, velocity, weights)


def body(
    density,
    velocity,
    shear_rates,
    hermite_matrix,
    laguerre_matrix,
    flow_first,
    flow_second,
    stress_weights,
):
    rows = density.reshape(ROWS, 128)
    speeds = velocity.reshape(8, 128)
    shear = shear_rates.reshape(16, 128)
    first = jnp.transpose(flow_first, (1, 0, 2)).reshape(40, 10)
    second = jnp.transpose(flow_second, (1, 0, 2)).reshape(40, 10)
    weights = jnp.transpose(stress_weights.reshape(3, 5, MODES_P), (1, 2, 0))
    place = (lax.axis_index("col") * 5).astype(jnp.int32).reshape(1)

    count_x = lax.axis_size("gx")
    count_y = lax.axis_size("gy")
    ring = [(i, (i + 1) % count_x) for i in range(count_x)]
    back = [(target, source) for source, target in ring]
    line = [(i, i + 1) for i in range(count_y - 1)]
    line_back = [(target, source) for source, target in line]

    low, high = x_halos(rows)
    left = lax.ppermute(high, "gx", ring)
    right = lax.ppermute(low, "gx", back)
    edge_low, edge_high = y_edges(rows)
    below = lax.ppermute(edge_high, "gy", line)
    above = lax.ppermute(edge_low, "gy", line_back)
    other = lax.ppermute(rows, "col", [(0, 1), (1, 0)])
    partial = main(place, laguerre_matrix, rows, other, speeds, shear, first, second, hermite_matrix)
    advanced, stress = final(partial, left, right, below, above, speeds, weights)
    stress = lax.psum(stress, "col")
    return (advanced.reshape(density.shape), stress.reshape(3, 4, 128))


def solution(mesh):
    in_specs = (
        P("col", None, None, "gx", "gy"),
        P(None, "gx", "gy"),
        P(None, "gx", "gy"),
        P(),
        P(),
        P(),
        P(),
        P(None, "col", None, None),
    )
    out_specs = (P("col", None, None, "gx", "gy"), P(None, "gx", "gy"))
    return jax.shard_map(body, mesh=mesh, in_specs=in_specs, out_specs=out_specs, check_vma=False)
```

```python
import functools

import jax
import jax.numpy as jnp
from jax import lax
from jax.experimental import pallas as pl
from jax.experimental.pallas import tpu as pltpu
from jax.sharding import PartitionSpec as P

time_step = 0.1
highest = lax.Precision.HIGHEST
f32 = jnp.float32
bf16 = jnp.bfloat16

ROWS = 2000
PQ = 50
RX = 40
PQ_PAD = 56
K_HALF = 64
N_PAIR = 20
MODES_P = 100
MODES_PAD = 104


vmem = pl.BlockSpec(memory_space=pltpu.VMEM)
smem = pl.BlockSpec(memory_space=pltpu.SMEM)
hbm = pl.BlockSpec(memory_space=pl.ANY)


def upwind(speed):
    plus = jnp.maximum(speed, 0.0)
    minus = jnp.minimum(speed, 0.0)
    t = time_step
    center = (-1.5 * t) * jnp.abs(speed)
    return center, (2 * t) * plus, (-0.5 * t) * plus, (-2 * t) * minus, (0.5 * t) * minus


def tens(value):
    total = jnp.zeros_like(value)
    for j in range(1, 5):
        total = total + (value >= 10 * j).astype(jnp.int32)
    return total


def iota(shape, dim):
    return lax.broadcasted_iota(jnp.int32, shape, dim)


def one_hot(condition):
    return jnp.where(condition, 1.0, 0.0).astype(f32)


def halo_kernel(x_ref, low_ref, high_ref):
    for p in range(5):
        for k in range(2):
            low_ref[p, k, 0:MODES_P, :] = x_ref[pl.ds(400 * p + k, MODES_P, stride=4), :]
            high_ref[p, k, 0:MODES_P, :] = x_ref[pl.ds(400 * p + 2 + k, MODES_P, stride=4), :]


def x_halos(rows):
    shape = jax.ShapeDtypeStruct((5, 2, MODES_PAD, 128), f32)
    return pl.pallas_call(
        halo_kernel,
        in_specs=[vmem],
        out_specs=[vmem, vmem],
        out_shape=[shape, shape],
        cost_estimate=pl.CostEstimate(flops=0, bytes_accessed=2 * ROWS * 512, transcendentals=0),
        compiler_params=pltpu.CompilerParams(vmem_limit_bytes=16 << 20),
        name="x_halos",
    )(rows)


def edge_kernel(x_ref, low_ref, high_ref, rows_ref):
    for x in range(4):
        rows_ref[x * 128 + 96 : (x + 1) * 128, :] = jnp.zeros((32, 256), bf16)
    lane = lax.rem(iota((8, 256), 1), 128)
    row = iota((8, 256), 0)
    pick = one_hot(((row < 2) & (lane == row)) | ((row >= 2) & (row < 4) & (lane == row + 124))).astype(bf16)
    for p in range(5):
        for x in range(4):
            high, low = split(x_ref[pl.ds(400 * p + x, MODES_P, stride=4), :])
            rows_ref[x * 128 : x * 128 + MODES_P, 0:128] = high
            rows_ref[x * 128 : x * 128 + MODES_P, 128:256] = low
        edges = lax.dot_general(pick, rows_ref[...], (((1,), (1,)), ((), ())), preferred_element_type=f32)
        low_ref[:, p * 512 : (p + 1) * 512] = edges[0:2]
        high_ref[:, p * 512 : (p + 1) * 512] = edges[2:4]


def y_edges(rows):
    shape = jax.ShapeDtypeStruct((2, 5 * 512), f32)
    return pl.pallas_call(
        edge_kernel,
        in_specs=[vmem],
        out_specs=[vmem, vmem],
        out_shape=[shape, shape],
        scratch_shapes=[pltpu.VMEM((512, 256), bf16)],
        cost_estimate=pl.CostEstimate(flops=0, bytes_accessed=ROWS * 512, transcendentals=0),
        compiler_params=pltpu.CompilerParams(vmem_limit_bytes=16 << 20),
        name="y_edges",
    )(rows)


def split(value):
    high = value.astype(bf16)
    low = (value - high.astype(f32)).astype(bf16)
    return high, low


def coupling(start, first, second, hermite):
    rows = 5 * PQ_PAD

    def row_ids(width):
        i = iota((rows, width), 0)
        c = jnp.zeros_like(i)
        for j in range(1, 5):
            c = c + (i >= PQ_PAD * j).astype(jnp.int32)
        ab = i - PQ_PAD * c
        a = tens(ab)
        return c, a + start, ab - 10 * a, ab < PQ

    def expand(table, index, c, valid):
        t40 = iota((rows, 40), 1)
        t10 = iota((rows, 10), 1)
        c40, a40, b40, ok40 = row_ids(40)
        c10, a10, b10, ok10 = row_ids(10)
        i40 = a40 if index == 0 else b40
        i10 = a10 if index == 0 else b10
        pick_flow = one_hot(ok40 & (c40 < 4) & (t40 == 4 * i40 + c40))
        pick_spring = one_hot(ok10 & (c10 == 4) & (t10 == i10))
        return jnp.dot(pick_flow, table, precision=highest, preferred_element_type=f32) + jnp.dot(
            pick_spring, hermite, precision=highest, preferred_element_type=f32
        )

    def columns(height):
        k = iota((height, 128), 1)
        other = k >= K_HALF
        kk = jnp.where(other, k - K_HALF, k)
        p_here = tens(kk)
        p = p_here + jnp.where(other, 5 - start, start)
        return p, kk - 10 * p_here, kk < PQ

    c, a, b, valid = row_ids(128)
    p10, q10, ok10 = columns(10)
    source = iota((10, 128), 0)
    left = expand(first, 0, c, valid)
    right = expand(second, 1, c, valid)
    left = jnp.dot(left, one_hot(ok10 & (source == p10)), precision=highest, preferred_element_type=f32)
    right = jnp.dot(right, one_hot(ok10 & (source == q10)), precision=highest, preferred_element_type=f32)
    p, q, ok = columns(rows)
    spring = c == 4
    both = left * jnp.where(spring, one_hot(b == q), right)
    both = both + jnp.where(spring & (a == p), right, 0.0)
    return time_step * both


def main_kernel(
    place_ref,
    laguerre_ref,
    own_hbm,
    other_hbm,
    velocity_ref,
    shear_ref,
    first_ref,
    second_ref,
    hermite_ref,
    out_ref,
    own_ref,
    other_ref,
    turned_ref,
    rate_ref,
    result_ref,
    wide_ref,
    narrow_ref,
    coef_ref,
    sems,
):
    copy_own = pltpu.make_async_copy(own_hbm, own_ref.at[0:ROWS], sems.at[0])
    copy_other = pltpu.make_async_copy(other_hbm, other_ref.at[0:ROWS], sems.at[1])
    copy_own.start()
    copy_other.start()
    zeros = jnp.zeros((K_HALF * RX - ROWS, 128), f32)
    own_ref[ROWS:, :] = zeros
    other_ref[ROWS:, :] = zeros

    matrix = coupling(place_ref[0], first_ref[...], second_ref[...], hermite_ref[...])
    matrix_high, matrix_low = split(matrix)
    wide_ref[:, 0:128] = matrix_high
    wide_ref[:, 128:256] = matrix_high
    narrow_ref[...] = matrix_low

    u = velocity_ref[0:4, :]
    v = velocity_ref[4:8, :]
    lane = iota((4, 128), 1)
    u0, um1, um2, up1, up2 = upwind(u)
    v0, vm1, vm2, vp1, vp2 = upwind(v)
    coefs = (
        1.0 + u0 + v0,
        um1,
        um2,
        up1,
        up2,
        jnp.where(lane >= 1, vm1, 0.0),
        jnp.where(lane >= 2, vm2, 0.0),
        jnp.where(lane < 127, vp1, 0.0),
        jnp.where(lane < 126, vp2, 0.0),
    )
    for i, c in enumerate(coefs):
        coef_ref[i, 0:4, :] = c

    copy_own.wait()
    copy_other.wait()

    def pair(i, carry):
        parts = []
        for t in range(2):
            rx = 2 * i + t
            own = own_ref[pl.ds(rx, K_HALF, stride=RX), :]
            other = other_ref[pl.ds(rx, K_HALF, stride=RX), :]
            turned_ref[pl.ds(pl.multiple_of(rx * K_HALF, K_HALF), K_HALF), :] = own
            own_high, own_low = split(own)
            other_high, other_low = split(other)
            parts.append(jnp.concatenate([own_high, other_high, own_low, other_low], axis=0))
        data = jnp.concatenate(parts, axis=1)
        product = jnp.dot(wide_ref[...], data, preferred_element_type=f32)
        product = product + jnp.dot(narrow_ref[...], data[0:128], preferred_element_type=f32)
        for t in range(2):
            rx = 2 * i + t
            x = lax.rem(rx, 4)
            part = product[:, t * 128 : (t + 1) * 128]
            total = part[4 * PQ_PAD : 5 * PQ_PAD]
            for c in range(4):
                total = total + shear_ref[pl.ds(4 * c + x, 1), :] * part[c * PQ_PAD : (c + 1) * PQ_PAD]
            rate_ref[pl.ds(pl.multiple_of(rx * PQ_PAD, PQ_PAD), PQ_PAD), :] = total
        return carry

    lax.fori_loop(0, N_PAIR, pair, 0)

    def strip(j, carry):
        def field(r, x):
            return turned_ref[pl.ds(pl.multiple_of((4 * r + x) * K_HALF + 8 * j, 8), 8), :]

        for x in range(4):
            def coef(i):
                return coef_ref[i, x : x + 1, :]

            here = [field(r, x) for r in range(10)]
            for r in range(10):
                mixed = laguerre_ref[r, 0] * here[0]
                for s in range(1, 10):
                    mixed = mixed + laguerre_ref[r, s] * here[s]
                f = here[r]
                total = rate_ref[pl.ds(pl.multiple_of((4 * r + x) * PQ_PAD + 8 * j, 8), 8), :]
                total = total + time_step * mixed + coef(0) * f
                for shift, i in ((-1, 1), (-2, 2), (1, 3), (2, 4)):
                    if 0 <= x + shift < 4:
                        total = total + coef(i) * field(r, x + shift)
                for shift, i in ((1, 5), (2, 6), (127, 7), (126, 8)):
                    total = total + coef(i) * pltpu.roll(f, shift, 1)
                result_ref[pl.ds(j * (8 * RX) + 4 * r + x, 8, stride=RX), :] = total
        return carry

    lax.fori_loop(0, PQ_PAD // 8, strip, 0)
    copy_out = pltpu.make_async_copy(result_ref.at[0:ROWS], out_ref, sems.at[2])
    copy_out.start()
    copy_out.wait()


def main(place, laguerre, own, other, velocity, shear, first, second, hermite):
    return pl.pallas_call(
        main_kernel,
        in_specs=[smem, smem, hbm, hbm, vmem, vmem, vmem, vmem, vmem],
        out_specs=vmem,
        out_shape=jax.ShapeDtypeStruct((ROWS, 128), f32),
        scratch_shapes=[
            pltpu.VMEM((K_HALF * RX, 128), f32),
            pltpu.VMEM((K_HALF * RX, 128), f32),
            pltpu.VMEM((K_HALF * RX, 128), f32),
            pltpu.VMEM((PQ_PAD * RX, 128), f32),
            pltpu.VMEM((PQ_PAD * RX, 128), f32),
            pltpu.VMEM((5 * PQ_PAD, 256), bf16),
            pltpu.VMEM((5 * PQ_PAD, 128), bf16),
            pltpu.VMEM((9, 8, 128), f32),
            pltpu.SemaphoreType.DMA((3,)),
        ],
        compiler_params=pltpu.CompilerParams(vmem_limit_bytes=24 << 20),
        cost_estimate=pl.CostEstimate(flops=2 * 280 * 384 * 5120, bytes_accessed=3 * ROWS * 512, transcendentals=0),
        name="main_step",
    )(place, laguerre, own, other, velocity, shear, first, second, hermite)


def final_kernel(
    partial_ref, left_ref, right_ref, below_ref, above_ref, velocity_ref, weight_ref, out_hbm, stress_ref, out_ref, sems
):
    u = velocity_ref[0:4, :]
    v = velocity_ref[4:8, :]
    lane4 = iota((4, 128), 1)
    _, um1, um2, up1, up2 = upwind(u)
    _, vm1, vm2, vp1, vp2 = upwind(v)
    near = jnp.where(lane4 == 0, vm1, jnp.where(lane4 == 127, vp1, 0.0))
    far = jnp.where(lane4 <= 1, vm2, jnp.where(lane4 >= 126, vp2, 0.0))
    row = lax.rem(iota((32, 256), 0), 8)
    lane = iota((32, 256), 1)
    hit = (row == 1) & ((lane == 0) | (lane == 129))
    hit = hit | ((row == 2) & ((lane == 127) | (lane == 254)))
    hit = hit | ((row == 0) & (lane == 128))
    hit = hit | ((row == 3) & (lane == 255))
    place = one_hot(hit).astype(bf16)
    stress = [jnp.zeros((1, 128), f32) for _ in range(12)]
    copies = []
    for p in range(5):
        lanes = slice(p * 512, (p + 1) * 512)
        edges = jnp.concatenate([below_ref[:, lanes], above_ref[:, lanes], jnp.zeros((4, 512), f32)], axis=0)
        high = edges.astype(bf16).astype(f32)
        rest = edges - high
        middle = rest.astype(bf16).astype(f32)
        low = rest - middle
        stacked = jnp.concatenate([high, middle, low, jnp.zeros((8, 512), f32)], axis=0).astype(bf16)
        spread = lax.dot_general(stacked, place, (((0,), (0,)), ((), ())), preferred_element_type=f32)
        left_far = left_ref[p, 0, 0:MODES_P, :]
        left_near = left_ref[p, 1, 0:MODES_P, :]
        right_near = right_ref[p, 0, 0:MODES_P, :]
        right_far = right_ref[p, 1, 0:MODES_P, :]
        for x in range(4):
            total = partial_ref[pl.ds(400 * p + x, MODES_P, stride=4), :]
            total = total + near[x : x + 1] * spread[x * 128 : x * 128 + MODES_P, 0:128]
            total = total + far[x : x + 1] * spread[x * 128 : x * 128 + MODES_P, 128:256]
            if x == 0:
                total = total + um1[0:1] * left_near + um2[0:1] * left_far
            if x == 1:
                total = total + um2[1:2] * left_near
            if x == 2:
                total = total + up2[2:3] * right_near
            if x == 3:
                total = total + up1[3:4] * right_near + up2[3:4] * right_far
            out_ref[pl.ds(400 * p + x, MODES_P, stride=4), :] = total
            for s in range(3):
                moment = jnp.sum(weight_ref[p, :, s : s + 1] * total, axis=0, keepdims=True)
                stress[4 * s + x] = stress[4 * s + x] + moment
        rows = pl.ds(400 * p, 400)
        copies.append(pltpu.make_async_copy(out_ref.at[rows], out_hbm.at[rows], sems.at[p]))
        copies[-1].start()
    for s in range(3):
        for x in range(4):
            stress_ref[s, x : x + 1, :] = stress[4 * s + x]
    for copy in copies:
        copy.wait()


def final(partial, left, right, below, above, velocity, weights):
    return pl.pallas_call(
        final_kernel,
        in_specs=[vmem] * 7,
        out_specs=[hbm, vmem],
        out_shape=[jax.ShapeDtypeStruct((ROWS, 128), f32), jax.ShapeDtypeStruct((3, 4, 128), f32)],
        scratch_shapes=[pltpu.VMEM((ROWS, 128), f32), pltpu.SemaphoreType.DMA((5,))],
        cost_estimate=pl.CostEstimate(flops=20 * ROWS * 128, bytes_accessed=4 * ROWS * 512, transcendentals=0),
        compiler_params=pltpu.CompilerParams(vmem_limit_bytes=16 << 20),
        name="final_step",
    )(partial, left, right, below, above, velocity, weights)


def body(
    density,
    velocity,
    shear_rates,
    hermite_matrix,
    laguerre_matrix,
    flow_first,
    flow_second,
    stress_weights,
):
    rows = density.reshape(ROWS, 128)
    speeds = velocity.reshape(8, 128)
    shear = shear_rates.reshape(16, 128)
    first = jnp.transpose(flow_first, (1, 0, 2)).reshape(40, 10)
    second = jnp.transpose(flow_second, (1, 0, 2)).reshape(40, 10)
    weights = jnp.transpose(stress_weights.reshape(3, 5, MODES_P), (1, 2, 0))
    place = (lax.axis_index("col") * 5).astype(jnp.int32).reshape(1)

    count_x = lax.axis_size("gx")
    count_y = lax.axis_size("gy")
    ring = [(i, (i + 1) % count_x) for i in range(count_x)]
    back = [(target, source) for source, target in ring]
    line = [(i, i + 1) for i in range(count_y - 1)]
    line_back = [(target, source) for source, target in line]

    low, high = x_halos(rows)
    left = lax.ppermute(high, "gx", ring)
    right = lax.ppermute(low, "gx", back)
    edge_low, edge_high = y_edges(rows)
    below = lax.ppermute(edge_high, "gy", line)
    above = lax.ppermute(edge_low, "gy", line_back)
    other = lax.ppermute(rows, "col", [(0, 1), (1, 0)])
    partial = main(place, laguerre_matrix, rows, other, speeds, shear, first, second, hermite_matrix)
    advanced, stress = final(partial, left, right, below, above, speeds, weights)
    stress = lax.psum(stress, "col")
    return (advanced.reshape(density.shape), stress)


def solution(mesh):
    in_specs = (
        P("col", None, None, "gx", "gy"),
        P(None, "gx", "gy"),
        P(None, "gx", "gy"),
        P(),
        P(),
        P(),
        P(),
        P(None, "col", None, None),
    )
    out_specs = (P("col", None, None, "gx", "gy"), P(None, "gx", "gy"))
    return jax.shard_map(body, mesh=mesh, in_specs=in_specs, out_specs=out_specs, check_vma=False)
```

```python
import functools

import jax
import jax.numpy as jnp
from jax import lax
from jax.experimental import pallas as pl
from jax.experimental.pallas import tpu as pltpu
from jax.sharding import PartitionSpec as P

time_step = 0.1
highest = lax.Precision.HIGHEST
f32 = jnp.float32
bf16 = jnp.bfloat16

ROWS = 2000
PQ = 50
RX = 40
PQ_PAD = 56
K_HALF = 64
N_PAIR = 20
MODES_P = 100
MODES_PAD = 104
PACK_UNROLL = 40
PAIR_UNROLL = 20
STRIP_UNROLL = 1


vmem = pl.BlockSpec(memory_space=pltpu.VMEM)
smem = pl.BlockSpec(memory_space=pltpu.SMEM)
hbm = pl.BlockSpec(memory_space=pl.ANY)


def upwind(speed):
    plus = jnp.maximum(speed, 0.0)
    minus = jnp.minimum(speed, 0.0)
    t = time_step
    center = (-1.5 * t) * jnp.abs(speed)
    return center, (2 * t) * plus, (-0.5 * t) * plus, (-2 * t) * minus, (0.5 * t) * minus


def tens(value):
    total = jnp.zeros_like(value)
    for j in range(1, 5):
        total = total + (value >= 10 * j).astype(jnp.int32)
    return total


def iota(shape, dim):
    return lax.broadcasted_iota(jnp.int32, shape, dim)


def one_hot(condition):
    return jnp.where(condition, 1.0, 0.0).astype(f32)


def halo_kernel(x_ref, low_ref, high_ref):
    for p in range(5):
        for k in range(2):
            low_ref[p, k, 0:MODES_P, :] = x_ref[pl.ds(400 * p + k, MODES_P, stride=4), :]
            high_ref[p, k, 0:MODES_P, :] = x_ref[pl.ds(400 * p + 2 + k, MODES_P, stride=4), :]


def x_halos(rows):
    shape = jax.ShapeDtypeStruct((5, 2, MODES_PAD, 128), f32)
    return pl.pallas_call(
        halo_kernel,
        in_specs=[vmem],
        out_specs=[vmem, vmem],
        out_shape=[shape, shape],
        cost_estimate=pl.CostEstimate(flops=0, bytes_accessed=2 * ROWS * 512, transcendentals=0),
        compiler_params=pltpu.CompilerParams(vmem_limit_bytes=16 << 20),
        name="x_halos",
    )(rows)


def edge_kernel(x_ref, low_ref, high_ref, rows_ref):
    for x in range(4):
        rows_ref[x * 128 + 96 : (x + 1) * 128, :] = jnp.zeros((32, 256), bf16)
    lane = lax.rem(iota((8, 256), 1), 128)
    row = iota((8, 256), 0)
    pick = one_hot(((row < 2) & (lane == row)) | ((row >= 2) & (row < 4) & (lane == row + 124))).astype(bf16)
    for p in range(5):
        for x in range(4):
            high, low = split(x_ref[pl.ds(400 * p + x, MODES_P, stride=4), :])
            rows_ref[x * 128 : x * 128 + MODES_P, 0:128] = high
            rows_ref[x * 128 : x * 128 + MODES_P, 128:256] = low
        edges = lax.dot_general(pick, rows_ref[...], (((1,), (1,)), ((), ())), preferred_element_type=f32)
        low_ref[:, p * 512 : (p + 1) * 512] = edges[0:2]
        high_ref[:, p * 512 : (p + 1) * 512] = edges[2:4]


def y_edges(rows):
    shape = jax.ShapeDtypeStruct((2, 5 * 512), f32)
    return pl.pallas_call(
        edge_kernel,
        in_specs=[vmem],
        out_specs=[vmem, vmem],
        out_shape=[shape, shape],
        scratch_shapes=[pltpu.VMEM((512, 256), bf16)],
        cost_estimate=pl.CostEstimate(flops=0, bytes_accessed=ROWS * 512, transcendentals=0),
        compiler_params=pltpu.CompilerParams(vmem_limit_bytes=16 << 20),
        name="y_edges",
    )(rows)


def split(value):
    high = value.astype(bf16)
    low = (value - high.astype(f32)).astype(bf16)
    return high, low


def coupling(start, first, second, hermite):
    rows = 5 * PQ_PAD

    def row_ids(width):
        i = iota((rows, width), 0)
        c = jnp.zeros_like(i)
        for j in range(1, 5):
            c = c + (i >= PQ_PAD * j).astype(jnp.int32)
        ab = i - PQ_PAD * c
        a = tens(ab)
        return c, a + start, ab - 10 * a, ab < PQ

    def expand(table, index, c, valid):
        t40 = iota((rows, 40), 1)
        t10 = iota((rows, 10), 1)
        c40, a40, b40, ok40 = row_ids(40)
        c10, a10, b10, ok10 = row_ids(10)
        i40 = a40 if index == 0 else b40
        i10 = a10 if index == 0 else b10
        pick_flow = one_hot(ok40 & (c40 < 4) & (t40 == 4 * i40 + c40))
        pick_spring = one_hot(ok10 & (c10 == 4) & (t10 == i10))
        return jnp.dot(pick_flow, table, precision=highest, preferred_element_type=f32) + jnp.dot(
            pick_spring, hermite, precision=highest, preferred_element_type=f32
        )

    def columns(height):
        k = iota((height, 128), 1)
        other = k >= K_HALF
        kk = jnp.where(other, k - K_HALF, k)
        p_here = tens(kk)
        p = p_here + jnp.where(other, 5 - start, start)
        return p, kk - 10 * p_here, kk < PQ

    c, a, b, valid = row_ids(128)
    p10, q10, ok10 = columns(10)
    source = iota((10, 128), 0)
    left = expand(first, 0, c, valid)
    right = expand(second, 1, c, valid)
    left = jnp.dot(left, one_hot(ok10 & (source == p10)), precision=highest, preferred_element_type=f32)
    right = jnp.dot(right, one_hot(ok10 & (source == q10)), precision=highest, preferred_element_type=f32)
    p, q, ok = columns(rows)
    spring = c == 4
    both = left * jnp.where(spring, one_hot(b == q), right)
    both = both + jnp.where(spring & (a == p), right, 0.0)
    return time_step * both


def main_kernel(
    place_ref,
    laguerre_ref,
    own_ref,
    other_ref,
    velocity_ref,
    shear_ref,
    first_ref,
    second_ref,
    hermite_ref,
    out_ref,
    data_ref,
    turned_ref,
    rate_ref,
    wide_ref,
    narrow_ref,
    coef_ref,
):
    matrix = coupling(place_ref[0], first_ref[...], second_ref[...], hermite_ref[...])
    matrix_high, matrix_low = split(matrix)
    wide_ref[:, 0:128] = matrix_high
    wide_ref[:, 128:256] = matrix_high
    narrow_ref[...] = matrix_low

    u = velocity_ref[0:4, :]
    v = velocity_ref[4:8, :]
    lane = iota((4, 128), 1)
    u0, um1, um2, up1, up2 = upwind(u)
    v0, vm1, vm2, vp1, vp2 = upwind(v)
    coefs = (
        1.0 + u0 + v0,
        um1,
        um2,
        up1,
        up2,
        jnp.where(lane >= 1, vm1, 0.0),
        jnp.where(lane >= 2, vm2, 0.0),
        jnp.where(lane < 127, vp1, 0.0),
        jnp.where(lane < 126, vp2, 0.0),
    )
    for i, c in enumerate(coefs):
        coef_ref[i, 0:4, :] = c

    def pack(rx, carry):
        base = pl.multiple_of((rx // 2) * 256, 256)
        lanes = pl.ds(pl.multiple_of(lax.rem(rx, 2) * 128, 128), 128)
        for i, ref in enumerate((own_ref, other_ref)):
            value = ref[pl.ds(rx, PQ, stride=RX), :]
            if i == 0:
                turned_ref[pl.ds(pl.multiple_of(rx * PQ_PAD, 8), PQ), :] = value
            high, low = split(value)
            for k, part in ((64 * i, high), (128 + 64 * i, low)):
                rows = pl.ds(base + k + 48, 16)
                data_ref[rows, lanes] = jnp.zeros((16, 128), bf16)
                data_ref[pl.ds(base + k, PQ), lanes] = part
        return carry

    lax.fori_loop(0, RX, pack, 0, unroll=PACK_UNROLL)

    def pair(i, carry):
        data = data_ref[pl.ds(pl.multiple_of(i * 256, 256), 256), :]
        product = jnp.dot(wide_ref[...], data, preferred_element_type=f32)
        product = product + jnp.dot(narrow_ref[...], data[0:128], preferred_element_type=f32)
        for t in range(2):
            rx = 2 * i + t
            x = lax.rem(rx, 4)
            part = product[:, t * 128 : (t + 1) * 128]
            total = part[4 * PQ_PAD : 5 * PQ_PAD]
            for c in range(4):
                total = total + shear_ref[pl.ds(4 * c + x, 1), :] * part[c * PQ_PAD : (c + 1) * PQ_PAD]
            rate_ref[pl.ds(pl.multiple_of(rx * PQ_PAD, 8), PQ_PAD), :] = total
        return carry

    lax.fori_loop(0, N_PAIR, pair, 0, unroll=PAIR_UNROLL)

    def strip(j, count):
        def field(r, x):
            return turned_ref[pl.ds(pl.multiple_of((4 * r + x) * PQ_PAD + 8 * j, 8), 8), :]

        for x in range(4):
            def coef(i):
                return coef_ref[i, x : x + 1, :]

            here = [field(r, x) for r in range(10)]
            for r in range(10):
                mixed = laguerre_ref[r, 0] * here[0]
                for s in range(1, 10):
                    mixed = mixed + laguerre_ref[r, s] * here[s]
                f = here[r]
                total = rate_ref[pl.ds(pl.multiple_of((4 * r + x) * PQ_PAD + 8 * j, 8), 8), :]
                total = total + time_step * mixed + coef(0) * f
                for shift, i in ((-1, 1), (-2, 2), (1, 3), (2, 4)):
                    if 0 <= x + shift < 4:
                        total = total + coef(i) * field(r, x + shift)
                for shift, i in ((1, 5), (2, 6), (127, 7), (126, 8)):
                    total = total + coef(i) * pltpu.roll(f, shift, 1)
                out_ref[pl.ds(j * (8 * RX) + 4 * r + x, count, stride=RX), :] = total[0:count]

    def whole(j, carry):
        strip(j, 8)
        return carry

    lax.fori_loop(0, PQ // 8, whole, 0, unroll=STRIP_UNROLL)
    strip(PQ // 8, PQ % 8)


def main(place, laguerre, own, other, velocity, shear, first, second, hermite):
    return pl.pallas_call(
        main_kernel,
        in_specs=[smem, smem] + [vmem] * 7,
        out_specs=vmem,
        out_shape=jax.ShapeDtypeStruct((ROWS, 128), f32),
        scratch_shapes=[
            pltpu.VMEM((N_PAIR * 256, 256), bf16),
            pltpu.VMEM((PQ_PAD * RX, 128), f32),
            pltpu.VMEM((PQ_PAD * RX, 128), f32),
            pltpu.VMEM((5 * PQ_PAD, 256), bf16),
            pltpu.VMEM((5 * PQ_PAD, 128), bf16),
            pltpu.VMEM((9, 8, 128), f32),
        ],
        compiler_params=pltpu.CompilerParams(vmem_limit_bytes=24 << 20),
        cost_estimate=pl.CostEstimate(flops=2 * 280 * 384 * 5120, bytes_accessed=3 * ROWS * 512, transcendentals=0),
        name="main_step",
    )(place, laguerre, own, other, velocity, shear, first, second, hermite)


def final_kernel(
    partial_ref, left_ref, right_ref, below_ref, above_ref, velocity_ref, weight_ref, out_hbm, stress_ref, out_ref, sems
):
    u = velocity_ref[0:4, :]
    v = velocity_ref[4:8, :]
    lane4 = iota((4, 128), 1)
    _, um1, um2, up1, up2 = upwind(u)
    _, vm1, vm2, vp1, vp2 = upwind(v)
    near = jnp.where(lane4 == 0, vm1, jnp.where(lane4 == 127, vp1, 0.0))
    far = jnp.where(lane4 <= 1, vm2, jnp.where(lane4 >= 126, vp2, 0.0))
    row = lax.rem(iota((32, 256), 0), 8)
    lane = iota((32, 256), 1)
    hit = (row == 1) & ((lane == 0) | (lane == 129))
    hit = hit | ((row == 2) & ((lane == 127) | (lane == 254)))
    hit = hit | ((row == 0) & (lane == 128))
    hit = hit | ((row == 3) & (lane == 255))
    place = one_hot(hit).astype(bf16)
    stress = [jnp.zeros((1, 128), f32) for _ in range(12)]
    copies = []
    for p in range(5):
        lanes = slice(p * 512, (p + 1) * 512)
        edges = jnp.concatenate([below_ref[:, lanes], above_ref[:, lanes], jnp.zeros((4, 512), f32)], axis=0)
        high = edges.astype(bf16).astype(f32)
        rest = edges - high
        middle = rest.astype(bf16).astype(f32)
        low = rest - middle
        stacked = jnp.concatenate([high, middle, low, jnp.zeros((8, 512), f32)], axis=0).astype(bf16)
        spread = lax.dot_general(stacked, place, (((0,), (0,)), ((), ())), preferred_element_type=f32)
        left_far = left_ref[p, 0, 0:MODES_P, :]
        left_near = left_ref[p, 1, 0:MODES_P, :]
        right_near = right_ref[p, 0, 0:MODES_P, :]
        right_far = right_ref[p, 1, 0:MODES_P, :]
        for x in range(4):
            total = partial_ref[pl.ds(400 * p + x, MODES_P, stride=4), :]
            total = total + near[x : x + 1] * spread[x * 128 : x * 128 + MODES_P, 0:128]
            total = total + far[x : x + 1] * spread[x * 128 : x * 128 + MODES_P, 128:256]
            if x == 0:
                total = total + um1[0:1] * left_near + um2[0:1] * left_far
            if x == 1:
                total = total + um2[1:2] * left_near
            if x == 2:
                total = total + up2[2:3] * right_near
            if x == 3:
                total = total + up1[3:4] * right_near + up2[3:4] * right_far
            out_ref[pl.ds(400 * p + x, MODES_P, stride=4), :] = total
            for s in range(3):
                moment = jnp.sum(weight_ref[p, :, s : s + 1] * total, axis=0, keepdims=True)
                stress[4 * s + x] = stress[4 * s + x] + moment
        rows = pl.ds(400 * p, 400)
        copies.append(pltpu.make_async_copy(out_ref.at[rows], out_hbm.at[rows], sems.at[p]))
        copies[-1].start()
    for s in range(3):
        for x in range(4):
            stress_ref[s, x : x + 1, :] = stress[4 * s + x]
    for copy in copies:
        copy.wait()


def final(partial, left, right, below, above, velocity, weights):
    return pl.pallas_call(
        final_kernel,
        in_specs=[vmem] * 7,
        out_specs=[hbm, vmem],
        out_shape=[jax.ShapeDtypeStruct((ROWS, 128), f32), jax.ShapeDtypeStruct((3, 4, 128), f32)],
        scratch_shapes=[pltpu.VMEM((ROWS, 128), f32), pltpu.SemaphoreType.DMA((5,))],
        cost_estimate=pl.CostEstimate(flops=20 * ROWS * 128, bytes_accessed=4 * ROWS * 512, transcendentals=0),
        compiler_params=pltpu.CompilerParams(vmem_limit_bytes=16 << 20),
        name="final_step",
    )(partial, left, right, below, above, velocity, weights)


def body(
    density,
    velocity,
    shear_rates,
    hermite_matrix,
    laguerre_matrix,
    flow_first,
    flow_second,
    stress_weights,
):
    rows = density.reshape(ROWS, 128)
    speeds = velocity.reshape(8, 128)
    shear = shear_rates.reshape(16, 128)
    first = jnp.transpose(flow_first, (1, 0, 2)).reshape(40, 10)
    second = jnp.transpose(flow_second, (1, 0, 2)).reshape(40, 10)
    weights = jnp.transpose(stress_weights.reshape(3, 5, MODES_P), (1, 2, 0))
    place = (lax.axis_index("col") * 5).astype(jnp.int32).reshape(1)

    count_x = lax.axis_size("gx")
    count_y = lax.axis_size("gy")
    ring = [(i, (i + 1) % count_x) for i in range(count_x)]
    back = [(target, source) for source, target in ring]
    line = [(i, i + 1) for i in range(count_y - 1)]
    line_back = [(target, source) for source, target in line]

    low, high = x_halos(rows)
    left = lax.ppermute(high, "gx", ring)
    right = lax.ppermute(low, "gx", back)
    edge_low, edge_high = y_edges(rows)
    below = lax.ppermute(edge_high, "gy", line)
    above = lax.ppermute(edge_low, "gy", line_back)
    other = lax.ppermute(rows, "col", [(0, 1), (1, 0)])
    partial = main(place, laguerre_matrix, rows, other, speeds, shear, first, second, hermite_matrix)
    advanced, stress = final(partial, left, right, below, above, speeds, weights)
    stress = lax.psum(stress, "col")
    return (advanced.reshape(density.shape), stress)


def solution(mesh):
    in_specs = (
        P("col", None, None, "gx", "gy"),
        P(None, "gx", "gy"),
        P(None, "gx", "gy"),
        P(),
        P(),
        P(),
        P(),
        P(None, "col", None, None),
    )
    out_specs = (P("col", None, None, "gx", "gy"), P(None, "gx", "gy"))
    return jax.shard_map(body, mesh=mesh, in_specs=in_specs, out_specs=out_specs, check_vma=False)
```

```python
import functools

import jax
import jax.numpy as jnp
from jax import lax
from jax.experimental import pallas as pl
from jax.experimental.pallas import tpu as pltpu
from jax.sharding import PartitionSpec as P

time_step = 0.1
highest = lax.Precision.HIGHEST
f32 = jnp.float32
bf16 = jnp.bfloat16

ROWS = 2000
PQ = 50
RX = 40
PQ_PAD = 56
K_HALF = 64
N_PAIR = 20
MODES_P = 100
PACK_UNROLL = 40
PAIR_UNROLL = 20
STRIP_UNROLL = 1


vmem = pl.BlockSpec(memory_space=pltpu.VMEM)
hbm = pl.BlockSpec(memory_space=pl.ANY)


def upwind(speed):
    plus = jnp.maximum(speed, 0.0)
    minus = jnp.minimum(speed, 0.0)
    t = time_step
    center = (-1.5 * t) * jnp.abs(speed)
    return center, (2 * t) * plus, (-0.5 * t) * plus, (-2 * t) * minus, (0.5 * t) * minus


def tens(value):
    total = jnp.zeros_like(value)
    for j in range(1, 5):
        total = total + (value >= 10 * j).astype(jnp.int32)
    return total


def iota(shape, dim):
    return lax.broadcasted_iota(jnp.int32, shape, dim)


def one_hot(condition):
    return jnp.where(condition, 1.0, 0.0).astype(f32)


def halo_kernel(x_ref, one_ref, two_ref):
    odd = 1 - lax.rem(lax.axis_index("gx"), 2)
    for ref, offset in ((one_ref, 2 - 2 * odd), (two_ref, 2 * odd)):
        for p in range(5):
            for k in range(2):
                ref[pl.ds(MODES_P * (2 * p + k), MODES_P), :] = x_ref[pl.ds(400 * p + k + offset, MODES_P, stride=4), :]


def x_halos(rows):
    shape = jax.ShapeDtypeStruct((ROWS // 2, 128), f32)
    return pl.pallas_call(
        halo_kernel,
        in_specs=[vmem],
        out_specs=[vmem, vmem],
        out_shape=[shape, shape],
        cost_estimate=pl.CostEstimate(flops=0, bytes_accessed=2 * ROWS * 512, transcendentals=0),
        compiler_params=pltpu.CompilerParams(vmem_limit_bytes=16 << 20),
        name="x_halos",
    )(rows)


def edge_kernel(x_ref, *refs):
    small, (one_ref, two_ref), kept, (rows_ref,) = refs[:6], refs[6:8], refs[8:14], refs[14:]
    for source, target in zip(small, kept):
        target[...] = source[...]
    for x in range(4):
        rows_ref[x * 128 + 96 : (x + 1) * 128, :] = jnp.zeros((32, 256), bf16)
    lane = lax.rem(iota((8, 256), 1), 128)
    row = iota((8, 256), 0)
    row = jnp.where(lax.rem(lax.axis_index("gy"), 2) == 0, jnp.bitwise_xor(row, 2), row)
    pick = one_hot(((row < 2) & (lane == row)) | ((row >= 2) & (row < 4) & (lane == row + 124))).astype(bf16)
    for p in range(5):
        for x in range(4):
            high, low = split(x_ref[pl.ds(400 * p + x, MODES_P, stride=4), :])
            rows_ref[x * 128 : x * 128 + MODES_P, 0:128] = high
            rows_ref[x * 128 : x * 128 + MODES_P, 128:256] = low
        edges = lax.dot_general(pick, rows_ref[...], (((1,), (1,)), ((), ())), preferred_element_type=f32)
        one_ref[:, p * 512 : (p + 1) * 512] = edges[0:2]
        two_ref[:, p * 512 : (p + 1) * 512] = edges[2:4]


def y_edges(rows, small):
    shape = jax.ShapeDtypeStruct((2, 5 * 512), f32)
    outs = pl.pallas_call(
        edge_kernel,
        in_specs=[vmem] * 7,
        out_specs=[vmem] * 8,
        out_shape=[shape, shape] + [jax.ShapeDtypeStruct(a.shape, f32) for a in small],
        scratch_shapes=[pltpu.VMEM((512, 256), bf16)],
        cost_estimate=pl.CostEstimate(flops=0, bytes_accessed=ROWS * 512, transcendentals=0),
        compiler_params=pltpu.CompilerParams(vmem_limit_bytes=16 << 20),
        name="y_edges",
    )(rows, *small)
    return outs[0], outs[1], outs[2:]


def split(value):
    high = value.astype(bf16)
    low = (value - high.astype(f32)).astype(bf16)
    return high, low


def exact(pick, table):
    high, low = split(table)
    rest = (table - high.astype(f32) - low.astype(f32)).astype(bf16)
    total = jnp.dot(pick, high, preferred_element_type=f32)
    total = total + jnp.dot(pick, low, preferred_element_type=f32)
    return total + jnp.dot(pick, rest, preferred_element_type=f32)


def coupling(start, first, second, hermite):
    rows = 5 * PQ_PAD

    def row_ids(width):
        i = iota((rows, width), 0)
        c = jnp.zeros_like(i)
        for j in range(1, 5):
            c = c + (i >= PQ_PAD * j).astype(jnp.int32)
        ab = i - PQ_PAD * c
        a = tens(ab)
        return c, a + start, ab - 10 * a, ab < PQ

    def columns(height):
        k = iota((height, 128), 1)
        other = k >= K_HALF
        kk = jnp.where(other, k - K_HALF, k)
        p_here = tens(kk)
        p = p_here + jnp.where(other, 5 - start, start)
        return p, kk - 10 * p_here, kk < PQ

    p10, q10, ok10 = columns(10)
    source = iota((10, 128), 0)
    spread_p = one_hot(ok10 & (source == p10))
    spread_q = one_hot(ok10 & (source == q10))

    def table(flow, spread):
        return jnp.concatenate(
            [
                jnp.dot(flow, spread, precision=highest, preferred_element_type=f32),
                jnp.dot(hermite, spread, precision=highest, preferred_element_type=f32),
                jnp.zeros((6, 128), f32),
            ],
            axis=0,
        )

    c, a, b, valid = row_ids(56)
    t = iota((rows, 56), 1)
    pick_a = one_hot(valid & (t == jnp.where(c == 4, 40 + a, 4 * a + c))).astype(bf16)
    pick_b = one_hot(valid & (t == jnp.where(c == 4, 40 + b, 4 * b + c))).astype(bf16)
    left = exact(pick_a, table(first, spread_p))
    right = exact(pick_b, table(second, spread_q))
    c, a, b, _ = row_ids(128)
    p, q, _ = columns(rows)
    spring = c == 4
    both = left * jnp.where(spring, one_hot(b == q), right)
    both = both + jnp.where(spring & (a == p), right, 0.0)
    return time_step * both


def main_kernel(
    laguerre_ref,
    own_ref,
    other_ref,
    velocity_ref,
    shear_ref,
    first_ref,
    second_ref,
    hermite_ref,
    out_ref,
    data_ref,
    turned_ref,
    rate_ref,
    wide_ref,
    narrow_ref,
    coef_ref,
    mix_ref,
):
    matrix = coupling(5 * lax.axis_index("col"), first_ref[...], second_ref[...], hermite_ref[...])
    matrix_high, matrix_low = split(matrix)
    wide_ref[:, 0:128] = matrix_high
    wide_ref[:, 128:256] = matrix_high
    narrow_ref[...] = matrix_low

    u = velocity_ref[0:4, :]
    v = velocity_ref[4:8, :]
    lane = iota((4, 128), 1)
    u0, um1, um2, up1, up2 = upwind(u)
    v0, vm1, vm2, vp1, vp2 = upwind(v)
    coefs = (
        1.0 + u0 + v0,
        um1,
        um2,
        up1,
        up2,
        jnp.where(lane >= 1, vm1, 0.0),
        jnp.where(lane >= 2, vm2, 0.0),
        jnp.where(lane < 127, vp1, 0.0),
        jnp.where(lane < 126, vp2, 0.0),
    )
    for i, c in enumerate(coefs):
        coef_ref[i, 0:4, :] = c
    laguerre = time_step * laguerre_ref[...]
    for r in range(10):
        for s in range(10):
            mix_ref[10 * r + s] = jnp.broadcast_to(laguerre[r : r + 1, s : s + 1], (8, 128))

    def pack(rx, carry):
        base = pl.multiple_of((rx // 2) * 256, 256)
        lanes = pl.ds(pl.multiple_of(lax.rem(rx, 2) * 128, 128), 128)
        for i, ref in enumerate((own_ref, other_ref)):
            value = ref[pl.ds(rx, PQ, stride=RX), :]
            if i == 0:
                turned_ref[pl.ds(pl.multiple_of(rx * PQ_PAD, 8), PQ), :] = value
            high, low = split(value)
            for k, part in ((64 * i, high), (128 + 64 * i, low)):
                rows = pl.ds(base + k + 48, 16)
                data_ref[rows, lanes] = jnp.zeros((16, 128), bf16)
                data_ref[pl.ds(base + k, PQ), lanes] = part
        return carry

    lax.fori_loop(0, RX, pack, 0, unroll=PACK_UNROLL)

    def pair(i, carry):
        data = data_ref[pl.ds(pl.multiple_of(i * 256, 256), 256), :]
        product = jnp.dot(wide_ref[...], data, preferred_element_type=f32)
        product = product + jnp.dot(narrow_ref[...], data[0:128], preferred_element_type=f32)
        for t in range(2):
            rx = 2 * i + t
            x = lax.rem(rx, 4)
            part = product[:, t * 128 : (t + 1) * 128]
            total = part[4 * PQ_PAD : 5 * PQ_PAD]
            for c in range(4):
                total = total + shear_ref[pl.ds(4 * c + x, 1), :] * part[c * PQ_PAD : (c + 1) * PQ_PAD]
            rate_ref[pl.ds(pl.multiple_of(rx * PQ_PAD, 8), PQ_PAD), :] = total
        return carry

    lax.fori_loop(0, N_PAIR, pair, 0, unroll=PAIR_UNROLL)

    def strip(j, count):
        def field(r, x):
            return turned_ref[pl.ds(pl.multiple_of((4 * r + x) * PQ_PAD + 8 * j, 8), 8), :]

        def coef(i, x):
            return coef_ref[i, x : x + 1, :]

        for half in ((0, 1), (2, 3)):
            here = {x: [field(r, x) for r in range(10)] for x in half}
            for r in range(10):
                mix = [mix_ref[10 * r + s] for s in range(10)]
                for x in half:
                    f = here[x][r]
                    total = rate_ref[pl.ds(pl.multiple_of((4 * r + x) * PQ_PAD + 8 * j, 8), 8), :]
                    total = total + coef(0, x) * f
                    for s in range(10):
                        total = total + mix[s] * here[x][s]
                    for shift, i in ((-1, 1), (-2, 2), (1, 3), (2, 4)):
                        if 0 <= x + shift < 4:
                            total = total + coef(i, x) * field(r, x + shift)
                    for shift, i in ((1, 5), (2, 6), (127, 7), (126, 8)):
                        total = total + coef(i, x) * pltpu.roll(f, shift, 1)
                    out_ref[pl.ds(j * (8 * RX) + 4 * r + x, count, stride=RX), :] = total[0:count]

    def whole(j, carry):
        strip(j, 8)
        return carry

    lax.fori_loop(0, PQ // 8, whole, 0, unroll=STRIP_UNROLL)
    strip(PQ // 8, PQ % 8)


def main(laguerre, own, other, velocity, shear, first, second, hermite):
    return pl.pallas_call(
        main_kernel,
        in_specs=[vmem] * 8,
        out_specs=vmem,
        out_shape=jax.ShapeDtypeStruct((ROWS, 128), f32),
        scratch_shapes=[
            pltpu.VMEM((N_PAIR * 256, 256), bf16),
            pltpu.VMEM((PQ_PAD * RX, 128), f32),
            pltpu.VMEM((PQ_PAD * RX, 128), f32),
            pltpu.VMEM((5 * PQ_PAD, 256), bf16),
            pltpu.VMEM((5 * PQ_PAD, 128), bf16),
            pltpu.VMEM((9, 8, 128), f32),
            pltpu.VMEM((100, 8, 128), f32),
        ],
        compiler_params=pltpu.CompilerParams(vmem_limit_bytes=24 << 20),
        cost_estimate=pl.CostEstimate(flops=2 * 280 * 384 * 5120, bytes_accessed=3 * ROWS * 512, transcendentals=0),
        name="main_step",
    )(laguerre, own, other, velocity, shear, first, second, hermite)


def final_kernel(
    partial_ref,
    x_one_ref,
    x_two_ref,
    y_one_ref,
    y_two_ref,
    velocity_ref,
    weight_ref,
    out_hbm,
    stress_ref,
    out_ref,
    sems,
):
    odd_x = lax.rem(lax.axis_index("gx"), 2) == 0
    odd_y = lax.rem(lax.axis_index("gy"), 2) == 1

    def halo(on_left, p, k):
        layer = pl.ds(MODES_P * (2 * p + k), MODES_P)
        one, two = x_one_ref[layer, :], x_two_ref[layer, :]
        return jnp.where(odd_x, one, two) if on_left else jnp.where(odd_x, two, one)

    u = velocity_ref[0:4, :]
    v = velocity_ref[4:8, :]
    lane4 = iota((4, 128), 1)
    _, um1, um2, up1, up2 = upwind(u)
    _, vm1, vm2, vp1, vp2 = upwind(v)
    near = jnp.where(lane4 == 0, vm1, jnp.where(lane4 == 127, vp1, 0.0))
    far = jnp.where(lane4 <= 1, vm2, jnp.where(lane4 >= 126, vp2, 0.0))
    row = lax.rem(iota((32, 256), 0), 8)
    lane = iota((32, 256), 1)
    hit = (row == 1) & ((lane == 0) | (lane == 129))
    hit = hit | ((row == 2) & ((lane == 127) | (lane == 254)))
    hit = hit | ((row == 0) & (lane == 128))
    hit = hit | ((row == 3) & (lane == 255))
    place = one_hot(hit).astype(bf16)
    stress = [jnp.zeros((1, 128), f32) for _ in range(12)]
    copies = []
    for p in range(5):
        lanes = slice(p * 512, (p + 1) * 512)
        y_one = y_one_ref[:, lanes]
        y_two = y_two_ref[:, lanes]
        below = jnp.where(odd_y, y_one, y_two)
        above = jnp.where(odd_y, y_two, y_one)
        edges = jnp.concatenate([below, above, jnp.zeros((4, 512), f32)], axis=0)
        high = edges.astype(bf16).astype(f32)
        rest = edges - high
        middle = rest.astype(bf16).astype(f32)
        low = rest - middle
        stacked = jnp.concatenate([high, middle, low, jnp.zeros((8, 512), f32)], axis=0).astype(bf16)
        spread = lax.dot_general(stacked, place, (((0,), (0,)), ((), ())), preferred_element_type=f32)
        left_far = halo(True, p, 0)
        left_near = halo(True, p, 1)
        right_near = halo(False, p, 0)
        right_far = halo(False, p, 1)
        for x in range(4):
            total = partial_ref[pl.ds(400 * p + x, MODES_P, stride=4), :]
            total = total + near[x : x + 1] * spread[x * 128 : x * 128 + MODES_P, 0:128]
            total = total + far[x : x + 1] * spread[x * 128 : x * 128 + MODES_P, 128:256]
            if x == 0:
                total = total + um1[0:1] * left_near + um2[0:1] * left_far
            if x == 1:
                total = total + um2[1:2] * left_near
            if x == 2:
                total = total + up2[2:3] * right_near
            if x == 3:
                total = total + up1[3:4] * right_near + up2[3:4] * right_far
            out_ref[pl.ds(400 * p + x, MODES_P, stride=4), :] = total
            for s in range(3):
                moment = jnp.sum(weight_ref[p, :, s : s + 1] * total, axis=0, keepdims=True)
                stress[4 * s + x] = stress[4 * s + x] + moment
        rows = pl.ds(400 * p, 400)
        copies.append(pltpu.make_async_copy(out_ref.at[rows], out_hbm.at[rows], sems.at[p]))
        copies[-1].start()
    for s in range(3):
        for x in range(4):
            stress_ref[s, x : x + 1, :] = stress[4 * s + x]
    for copy in copies:
        copy.wait()


def final(partial, x_one, x_two, y_one, y_two, velocity, weights):
    return pl.pallas_call(
        final_kernel,
        in_specs=[vmem] * 7,
        out_specs=[hbm, vmem],
        out_shape=[jax.ShapeDtypeStruct((ROWS, 128), f32), jax.ShapeDtypeStruct((3, 4, 128), f32)],
        scratch_shapes=[pltpu.VMEM((ROWS, 128), f32), pltpu.SemaphoreType.DMA((5,))],
        cost_estimate=pl.CostEstimate(flops=20 * ROWS * 128, bytes_accessed=4 * ROWS * 512, transcendentals=0),
        compiler_params=pltpu.CompilerParams(vmem_limit_bytes=16 << 20),
        name="final_step",
    )(partial, x_one, x_two, y_one, y_two, velocity, weights)


def body(
    density,
    velocity,
    shear_rates,
    hermite_matrix,
    laguerre_matrix,
    flow_first,
    flow_second,
    stress_weights,
):
    rows = density.reshape(ROWS, 128)
    speeds = velocity.reshape(8, 128)
    shear = shear_rates.reshape(16, 128)
    first = jnp.transpose(flow_first, (1, 0, 2)).reshape(40, 10)
    second = jnp.transpose(flow_second, (1, 0, 2)).reshape(40, 10)
    weights = jnp.transpose(stress_weights.reshape(3, 5, MODES_P), (1, 2, 0))
    def pairings(axis, periodic):
        count = lax.axis_size(axis)
        one = [(i, i + 1) for i in range(0, count, 2)]
        two = [(i, (i + 1) % count) for i in range(1, count if periodic else count - 1, 2)]
        return [pairs + [(b, a) for a, b in pairs] for pairs in (one, two)]

    ring_two, ring_one = pairings("gx", True)
    line_one, line_two = pairings("gy", False)
    send_one, send_two = x_halos(rows)
    x_one = lax.ppermute(send_one, "gx", ring_one)
    x_two = lax.ppermute(send_two, "gx", ring_two)
    small = (speeds, shear, first, second, hermite_matrix, laguerre_matrix)
    send_one, send_two, small = y_edges(rows, small)
    speeds, shear, first, second, hermite_matrix, laguerre_matrix = small
    y_one = lax.ppermute(send_one, "gy", line_one)
    y_two = lax.ppermute(send_two, "gy", line_two)
    other = lax.ppermute(rows, "col", [(0, 1), (1, 0)])
    partial = main(laguerre_matrix, rows, other, speeds, shear, first, second, hermite_matrix)
    advanced, stress = final(partial, x_one, x_two, y_one, y_two, speeds, weights)
    stress = lax.psum(stress, "col")
    return (advanced.reshape(density.shape), stress)


def solution(mesh):
    in_specs = (
        P("col", None, None, "gx", "gy"),
        P(None, "gx", "gy"),
        P(None, "gx", "gy"),
        P(),
        P(),
        P(),
        P(),
        P(None, "col", None, None),
    )
    out_specs = (P("col", None, None, "gx", "gy"), P(None, "gx", "gy"))
    return jax.shard_map(body, mesh=mesh, in_specs=in_specs, out_specs=out_specs, check_vma=False)
```

```python
import functools

import jax
import jax.numpy as jnp
from jax import lax
from jax.experimental import pallas as pl
from jax.experimental.pallas import tpu as pltpu
from jax.sharding import PartitionSpec as P

time_step = 0.1
highest = lax.Precision.HIGHEST
f32 = jnp.float32
bf16 = jnp.bfloat16

ROWS = 2000
PQ = 50
RX = 40
PQ_PAD = 56
K_HALF = 64
N_PAIR = 20
MODES_P = 100
PACK_UNROLL = 40
PAIR_UNROLL = 20
STRIP_UNROLL = 1


vmem = pl.BlockSpec(memory_space=pltpu.VMEM)
hbm = pl.BlockSpec(memory_space=pl.ANY)


def upwind(speed):
    plus = jnp.maximum(speed, 0.0)
    minus = jnp.minimum(speed, 0.0)
    t = time_step
    center = (-1.5 * t) * jnp.abs(speed)
    return center, (2 * t) * plus, (-0.5 * t) * plus, (-2 * t) * minus, (0.5 * t) * minus


def tens(value):
    total = jnp.zeros_like(value)
    for j in range(1, 5):
        total = total + (value >= 10 * j).astype(jnp.int32)
    return total


def iota(shape, dim):
    return lax.broadcasted_iota(jnp.int32, shape, dim)


def one_hot(condition):
    return jnp.where(condition, 1.0, 0.0).astype(f32)


def halo_kernel(x_hbm, one_hbm, two_hbm, x_ref, one_ref, two_ref, in_sems, out_sems):
    odd = 1 - lax.rem(lax.axis_index("gx"), 2)
    loads = []
    stores = []
    for p in range(5):
        rows = pl.ds(400 * p, 400)
        loads.append(pltpu.make_async_copy(x_hbm.at[rows], x_ref.at[rows], in_sems.at[p]))
        loads[p].start()
    for p in range(5):
        loads[p].wait()
        layers = pl.ds(2 * MODES_P * p, 2 * MODES_P)
        for i, (ref, target, offset) in enumerate(
            ((one_ref, one_hbm, 2 - 2 * odd), (two_ref, two_hbm, 2 * odd))
        ):
            for k in range(2):
                ref[x_halo_rows(p, k), :] = x_ref[pl.ds(400 * p + k + offset, MODES_P, stride=4), :]
            stores.append(pltpu.make_async_copy(ref.at[layers], target.at[layers], out_sems.at[2 * p + i]))
            stores[-1].start()
    for store in stores:
        store.wait()


def x_halo_rows(p, k):
    return pl.ds(MODES_P * (2 * p + k), MODES_P)


def x_halos(rows):
    shape = jax.ShapeDtypeStruct((ROWS // 2, 128), f32)
    half = pltpu.VMEM((ROWS // 2, 128), f32)
    return pl.pallas_call(
        halo_kernel,
        in_specs=[hbm],
        out_specs=[hbm, hbm],
        out_shape=[shape, shape],
        scratch_shapes=[
            pltpu.VMEM((ROWS, 128), f32),
            half,
            half,
            pltpu.SemaphoreType.DMA((5,)),
            pltpu.SemaphoreType.DMA((10,)),
        ],
        cost_estimate=pl.CostEstimate(flops=0, bytes_accessed=2 * ROWS * 512, transcendentals=0),
        compiler_params=pltpu.CompilerParams(vmem_limit_bytes=16 << 20),
        name="x_halos",
    )(pltpu.with_memory_space_constraint(rows, pltpu.HBM))


def edge_kernel(x_ref, one_ref, two_ref, rows_ref):
    for x in range(4):
        rows_ref[x * 128 + 96 : (x + 1) * 128, :] = jnp.zeros((32, 256), bf16)
    lane = lax.rem(iota((8, 256), 1), 128)
    row = iota((8, 256), 0)
    row = jnp.where(lax.rem(lax.axis_index("gy"), 2) == 0, jnp.bitwise_xor(row, 2), row)
    pick = one_hot(((row < 2) & (lane == row)) | ((row >= 2) & (row < 4) & (lane == row + 124))).astype(bf16)
    for p in range(5):
        for x in range(4):
            high, low = split(x_ref[pl.ds(400 * p + x, MODES_P, stride=4), :])
            rows_ref[x * 128 : x * 128 + MODES_P, 0:128] = high
            rows_ref[x * 128 : x * 128 + MODES_P, 128:256] = low
        edges = lax.dot_general(pick, rows_ref[...], (((1,), (1,)), ((), ())), preferred_element_type=f32)
        one_ref[:, p * 512 : (p + 1) * 512] = edges[0:2]
        two_ref[:, p * 512 : (p + 1) * 512] = edges[2:4]


def y_edges(rows):
    shape = jax.ShapeDtypeStruct((2, 5 * 512), f32)
    return pl.pallas_call(
        edge_kernel,
        in_specs=[vmem],
        out_specs=[vmem, vmem],
        out_shape=[shape, shape],
        scratch_shapes=[pltpu.VMEM((512, 256), bf16)],
        cost_estimate=pl.CostEstimate(flops=0, bytes_accessed=ROWS * 512, transcendentals=0),
        compiler_params=pltpu.CompilerParams(vmem_limit_bytes=16 << 20),
        name="y_edges",
    )(rows)


def split(value):
    high = value.astype(bf16)
    low = (value - high.astype(f32)).astype(bf16)
    return high, low


def exact(pick, table):
    high, low = split(table)
    rest = (table - high.astype(f32) - low.astype(f32)).astype(bf16)
    total = jnp.dot(pick, high, preferred_element_type=f32)
    total = total + jnp.dot(pick, low, preferred_element_type=f32)
    return total + jnp.dot(pick, rest, preferred_element_type=f32)


def coupling(start, first, second, hermite):
    rows = 5 * PQ_PAD

    def row_ids(width):
        i = iota((rows, width), 0)
        c = jnp.zeros_like(i)
        for j in range(1, 5):
            c = c + (i >= PQ_PAD * j).astype(jnp.int32)
        ab = i - PQ_PAD * c
        a = tens(ab)
        return c, a + start, ab - 10 * a, ab < PQ

    def columns(height):
        k = iota((height, 128), 1)
        other = k >= K_HALF
        kk = jnp.where(other, k - K_HALF, k)
        p_here = tens(kk)
        p = p_here + jnp.where(other, 5 - start, start)
        return p, kk - 10 * p_here, kk < PQ

    p10, q10, ok10 = columns(10)
    source = iota((10, 128), 0)
    spread_p = one_hot(ok10 & (source == p10))
    spread_q = one_hot(ok10 & (source == q10))

    def table(flow, spread):
        return jnp.concatenate(
            [
                jnp.dot(flow, spread, precision=highest, preferred_element_type=f32),
                jnp.dot(hermite, spread, precision=highest, preferred_element_type=f32),
                jnp.zeros((6, 128), f32),
            ],
            axis=0,
        )

    c, a, b, valid = row_ids(56)
    t = iota((rows, 56), 1)
    pick_a = one_hot(valid & (t == jnp.where(c == 4, 40 + a, 4 * a + c))).astype(bf16)
    pick_b = one_hot(valid & (t == jnp.where(c == 4, 40 + b, 4 * b + c))).astype(bf16)
    left = exact(pick_a, table(first, spread_p))
    right = exact(pick_b, table(second, spread_q))
    c, a, b, _ = row_ids(128)
    p, q, _ = columns(rows)
    spring = c == 4
    both = left * jnp.where(spring, one_hot(b == q), right)
    both = both + jnp.where(spring & (a == p), right, 0.0)
    return time_step * both


def main_kernel(
    laguerre_ref,
    own_ref,
    other_ref,
    velocity_ref,
    shear_ref,
    first_ref,
    second_ref,
    hermite_ref,
    out_ref,
    data_ref,
    turned_ref,
    rate_ref,
    wide_ref,
    narrow_ref,
    coef_ref,
    mix_ref,
):
    matrix = coupling(5 * lax.axis_index("col"), first_ref[...], second_ref[...], hermite_ref[...])
    matrix_high, matrix_low = split(matrix)
    wide_ref[:, 0:128] = matrix_high
    wide_ref[:, 128:256] = matrix_high
    narrow_ref[...] = matrix_low

    u = velocity_ref[0:4, :]
    v = velocity_ref[4:8, :]
    lane = iota((4, 128), 1)
    u0, um1, um2, up1, up2 = upwind(u)
    v0, vm1, vm2, vp1, vp2 = upwind(v)
    coefs = (
        1.0 + u0 + v0,
        um1,
        um2,
        up1,
        up2,
        jnp.where(lane >= 1, vm1, 0.0),
        jnp.where(lane >= 2, vm2, 0.0),
        jnp.where(lane < 127, vp1, 0.0),
        jnp.where(lane < 126, vp2, 0.0),
    )
    for i, c in enumerate(coefs):
        coef_ref[i, 0:4, :] = c
    laguerre = time_step * laguerre_ref[...]
    for r in range(10):
        for s in range(10):
            mix_ref[10 * r + s] = jnp.broadcast_to(laguerre[r : r + 1, s : s + 1], (8, 128))

    def pack(rx, carry):
        base = pl.multiple_of((rx // 2) * 256, 256)
        lanes = pl.ds(pl.multiple_of(lax.rem(rx, 2) * 128, 128), 128)
        for i, ref in enumerate((own_ref, other_ref)):
            value = ref[pl.ds(rx, PQ, stride=RX), :]
            if i == 0:
                turned_ref[pl.ds(pl.multiple_of(rx * PQ_PAD, 8), PQ), :] = value
            high, low = split(value)
            for k, part in ((64 * i, high), (128 + 64 * i, low)):
                rows = pl.ds(base + k + 48, 16)
                data_ref[rows, lanes] = jnp.zeros((16, 128), bf16)
                data_ref[pl.ds(base + k, PQ), lanes] = part
        return carry

    lax.fori_loop(0, RX, pack, 0, unroll=PACK_UNROLL)

    def pair(i, carry):
        data = data_ref[pl.ds(pl.multiple_of(i * 256, 256), 256), :]
        product = jnp.dot(wide_ref[...], data, preferred_element_type=f32)
        product = product + jnp.dot(narrow_ref[...], data[0:128], preferred_element_type=f32)
        for t in range(2):
            rx = 2 * i + t
            x = lax.rem(rx, 4)
            part = product[:, t * 128 : (t + 1) * 128]
            total = part[4 * PQ_PAD : 5 * PQ_PAD]
            for c in range(4):
                total = total + shear_ref[pl.ds(4 * c + x, 1), :] * part[c * PQ_PAD : (c + 1) * PQ_PAD]
            rate_ref[pl.ds(pl.multiple_of(rx * PQ_PAD, 8), PQ_PAD), :] = total
        return carry

    lax.fori_loop(0, N_PAIR, pair, 0, unroll=PAIR_UNROLL)

    def strip(j, count):
        def field(r, x):
            return turned_ref[pl.ds(pl.multiple_of((4 * r + x) * PQ_PAD + 8 * j, 8), 8), :]

        def coef(i, x):
            return coef_ref[i, x : x + 1, :]

        for half in ((0, 1), (2, 3)):
            here = {x: [field(r, x) for r in range(10)] for x in half}
            for r in range(10):
                mix = [mix_ref[10 * r + s] for s in range(10)]
                for x in half:
                    f = here[x][r]
                    total = rate_ref[pl.ds(pl.multiple_of((4 * r + x) * PQ_PAD + 8 * j, 8), 8), :]
                    total = total + coef(0, x) * f
                    for s in range(10):
                        total = total + mix[s] * here[x][s]
                    for shift, i in ((-1, 1), (-2, 2), (1, 3), (2, 4)):
                        if 0 <= x + shift < 4:
                            total = total + coef(i, x) * field(r, x + shift)
                    for shift, i in ((1, 5), (2, 6), (127, 7), (126, 8)):
                        total = total + coef(i, x) * pltpu.roll(f, shift, 1)
                    out_ref[pl.ds(j * (8 * RX) + 4 * r + x, count, stride=RX), :] = total[0:count]

    def whole(j, carry):
        strip(j, 8)
        return carry

    lax.fori_loop(0, PQ // 8, whole, 0, unroll=STRIP_UNROLL)
    strip(PQ // 8, PQ % 8)


def main(laguerre, own, other, velocity, shear, first, second, hermite):
    return pl.pallas_call(
        main_kernel,
        in_specs=[vmem] * 8,
        out_specs=vmem,
        out_shape=jax.ShapeDtypeStruct((ROWS, 128), f32),
        scratch_shapes=[
            pltpu.VMEM((N_PAIR * 256, 256), bf16),
            pltpu.VMEM((PQ_PAD * RX, 128), f32),
            pltpu.VMEM((PQ_PAD * RX, 128), f32),
            pltpu.VMEM((5 * PQ_PAD, 256), bf16),
            pltpu.VMEM((5 * PQ_PAD, 128), bf16),
            pltpu.VMEM((9, 8, 128), f32),
            pltpu.VMEM((100, 8, 128), f32),
        ],
        compiler_params=pltpu.CompilerParams(vmem_limit_bytes=24 << 20),
        cost_estimate=pl.CostEstimate(flops=2 * 280 * 384 * 5120, bytes_accessed=3 * ROWS * 512, transcendentals=0),
        name="main_step",
    )(laguerre, own, other, velocity, shear, first, second, hermite)


def final_kernel(
    partial_ref,
    x_one_ref,
    x_two_ref,
    y_one_ref,
    y_two_ref,
    velocity_ref,
    weight_ref,
    out_hbm,
    stress_ref,
    out_ref,
    sems,
):
    odd_x = lax.rem(lax.axis_index("gx"), 2) == 0
    odd_y = lax.rem(lax.axis_index("gy"), 2) == 1

    def halo(on_left, p, k):
        layer = x_halo_rows(p, k)
        one, two = x_one_ref[layer, :], x_two_ref[layer, :]
        return jnp.where(odd_x, one, two) if on_left else jnp.where(odd_x, two, one)

    u = velocity_ref[0:4, :]
    v = velocity_ref[4:8, :]
    lane4 = iota((4, 128), 1)
    _, um1, um2, up1, up2 = upwind(u)
    _, vm1, vm2, vp1, vp2 = upwind(v)
    near = jnp.where(lane4 == 0, vm1, jnp.where(lane4 == 127, vp1, 0.0))
    far = jnp.where(lane4 <= 1, vm2, jnp.where(lane4 >= 126, vp2, 0.0))
    row = lax.rem(iota((32, 256), 0), 8)
    lane = iota((32, 256), 1)
    hit = (row == 1) & ((lane == 0) | (lane == 129))
    hit = hit | ((row == 2) & ((lane == 127) | (lane == 254)))
    hit = hit | ((row == 0) & (lane == 128))
    hit = hit | ((row == 3) & (lane == 255))
    place = one_hot(hit).astype(bf16)
    copies = []
    for p in range(5):
        lanes = slice(p * 512, (p + 1) * 512)
        y_one = y_one_ref[:, lanes]
        y_two = y_two_ref[:, lanes]
        below = jnp.where(odd_y, y_one, y_two)
        above = jnp.where(odd_y, y_two, y_one)
        edges = jnp.concatenate([below, above, jnp.zeros((4, 512), f32)], axis=0)
        high = edges.astype(bf16).astype(f32)
        rest = edges - high
        middle = rest.astype(bf16).astype(f32)
        low = rest - middle
        stacked = jnp.concatenate([high, middle, low, jnp.zeros((8, 512), f32)], axis=0).astype(bf16)
        spread = lax.dot_general(stacked, place, (((0,), (0,)), ((), ())), preferred_element_type=f32)
        left_far = halo(True, p, 0)
        left_near = halo(True, p, 1)
        right_near = halo(False, p, 0)
        right_far = halo(False, p, 1)
        for x in range(4):
            total = partial_ref[pl.ds(400 * p + x, MODES_P, stride=4), :]
            total = total + near[x : x + 1] * spread[x * 128 : x * 128 + MODES_P, 0:128]
            total = total + far[x : x + 1] * spread[x * 128 : x * 128 + MODES_P, 128:256]
            if x == 0:
                total = total + um1[0:1] * left_near + um2[0:1] * left_far
            if x == 1:
                total = total + um2[1:2] * left_near
            if x == 2:
                total = total + up2[2:3] * right_near
            if x == 3:
                total = total + up1[3:4] * right_near + up2[3:4] * right_far
            out_ref[pl.ds(400 * p + x, MODES_P, stride=4), :] = total
        rows = pl.ds(400 * p, 400)
        copies.append(pltpu.make_async_copy(out_ref.at[rows], out_hbm.at[rows], sems.at[p]))
        copies[-1].start()
    for x in range(4):
        for s in range(3):
            moment = jnp.zeros((MODES_P, 128), f32)
            for p in range(5):
                moment = moment + weight_ref[p, :, s : s + 1] * out_ref[pl.ds(400 * p + x, MODES_P, stride=4), :]
            stress_ref[s, x : x + 1, :] = jnp.sum(moment, axis=0, keepdims=True)
    for copy in copies:
        copy.wait()


def final(partial, x_one, x_two, y_one, y_two, velocity, weights):
    return pl.pallas_call(
        final_kernel,
        in_specs=[vmem] * 7,
        out_specs=[hbm, vmem],
        out_shape=[jax.ShapeDtypeStruct((ROWS, 128), f32), jax.ShapeDtypeStruct((3, 4, 128), f32)],
        scratch_shapes=[pltpu.VMEM((ROWS, 128), f32), pltpu.SemaphoreType.DMA((5,))],
        cost_estimate=pl.CostEstimate(flops=20 * ROWS * 128, bytes_accessed=4 * ROWS * 512, transcendentals=0),
        compiler_params=pltpu.CompilerParams(vmem_limit_bytes=16 << 20),
        name="final_step",
    )(partial, x_one, x_two, y_one, y_two, velocity, weights)


def body(
    density,
    velocity,
    shear_rates,
    hermite_matrix,
    laguerre_matrix,
    flow_first,
    flow_second,
    stress_weights,
):
    rows = density.reshape(ROWS, 128)
    speeds = velocity.reshape(8, 128)
    shear = shear_rates.reshape(16, 128)
    first = jnp.transpose(flow_first, (1, 0, 2)).reshape(40, 10)
    second = jnp.transpose(flow_second, (1, 0, 2)).reshape(40, 10)
    weights = jnp.transpose(stress_weights.reshape(3, 5, MODES_P), (1, 2, 0))
    def pairings(axis, periodic):
        count = lax.axis_size(axis)
        one = [(i, i + 1) for i in range(0, count, 2)]
        two = [(i, (i + 1) % count) for i in range(1, count if periodic else count - 1, 2)]
        return [pairs + [(b, a) for a, b in pairs] for pairs in (one, two)]

    ring_two, ring_one = pairings("gx", True)
    line_one, line_two = pairings("gy", False)
    send_one, send_two = x_halos(rows)
    x_one = lax.ppermute(send_one, "gx", ring_one)
    x_two = lax.ppermute(send_two, "gx", ring_two)
    send_one, send_two = y_edges(rows)
    y_one = lax.ppermute(send_one, "gy", line_one)
    y_two = lax.ppermute(send_two, "gy", line_two)
    other = lax.ppermute(rows, "col", [(0, 1), (1, 0)])
    partial = main(laguerre_matrix, rows, other, speeds, shear, first, second, hermite_matrix)
    advanced, stress = final(partial, x_one, x_two, y_one, y_two, speeds, weights)
    stress = lax.psum(stress, "col")
    return (advanced.reshape(density.shape), stress)


def solution(mesh):
    in_specs = (
        P("col", None, None, "gx", "gy"),
        P(None, "gx", "gy"),
        P(None, "gx", "gy"),
        P(),
        P(),
        P(),
        P(),
        P(None, "col", None, None),
    )
    out_specs = (P("col", None, None, "gx", "gy"), P(None, "gx", "gy"))
    return jax.shard_map(body, mesh=mesh, in_specs=in_specs, out_specs=out_specs, check_vma=False)
```

```python
import functools

import jax
import jax.numpy as jnp
from jax import lax
from jax.experimental import pallas as pl
from jax.experimental.pallas import tpu as pltpu
from jax.sharding import PartitionSpec as P

time_step = 0.1
highest = lax.Precision.HIGHEST
f32 = jnp.float32
bf16 = jnp.bfloat16

ROWS = 2000
PQ = 50
RX = 40
PQ_PAD = 56
K_HALF = 64
N_PAIR = 20
MODES_P = 100
PACK_UNROLL = 40
PAIR_UNROLL = 20
STRIP_UNROLL = 1


vmem = pl.BlockSpec(memory_space=pltpu.VMEM)
hbm = pl.BlockSpec(memory_space=pl.ANY)


def upwind(speed):
    plus = jnp.maximum(speed, 0.0)
    minus = jnp.minimum(speed, 0.0)
    t = time_step
    center = (-1.5 * t) * jnp.abs(speed)
    return center, (2 * t) * plus, (-0.5 * t) * plus, (-2 * t) * minus, (0.5 * t) * minus


def tens(value):
    total = jnp.zeros_like(value)
    for j in range(1, 5):
        total = total + (value >= 10 * j).astype(jnp.int32)
    return total


def iota(shape, dim):
    return lax.broadcasted_iota(jnp.int32, shape, dim)


def one_hot(condition):
    return jnp.where(condition, 1.0, 0.0).astype(f32)


def halo_kernel(x_ref, one_ref, two_ref):
    odd = 1 - lax.rem(lax.axis_index("gx"), 2)
    for ref, offset in ((one_ref, 2 - 2 * odd), (two_ref, 2 * odd)):
        for p in range(5):
            for k in range(2):
                ref[pl.ds(MODES_P * (2 * p + k), MODES_P), :] = x_ref[pl.ds(400 * p + k + offset, MODES_P, stride=4), :]


def x_halos(rows):
    shape = jax.ShapeDtypeStruct((ROWS // 2, 128), f32)
    return pl.pallas_call(
        halo_kernel,
        in_specs=[vmem],
        out_specs=[vmem, vmem],
        out_shape=[shape, shape],
        cost_estimate=pl.CostEstimate(flops=0, bytes_accessed=2 * ROWS * 512, transcendentals=0),
        compiler_params=pltpu.CompilerParams(vmem_limit_bytes=16 << 20),
        name="x_halos",
    )(rows)


def edge_kernel(x_ref, one_ref, two_ref, rows_ref):
    for x in range(4):
        rows_ref[x * 128 + 96 : (x + 1) * 128, :] = jnp.zeros((32, 256), bf16)
    lane = lax.rem(iota((8, 256), 1), 128)
    row = iota((8, 256), 0)
    row = jnp.where(lax.rem(lax.axis_index("gy"), 2) == 0, jnp.bitwise_xor(row, 2), row)
    pick = one_hot(((row < 2) & (lane == row)) | ((row >= 2) & (row < 4) & (lane == row + 124))).astype(bf16)
    for p in range(5):
        for x in range(4):
            high, low = split(x_ref[pl.ds(400 * p + x, MODES_P, stride=4), :])
            rows_ref[x * 128 : x * 128 + MODES_P, 0:128] = high
            rows_ref[x * 128 : x * 128 + MODES_P, 128:256] = low
        edges = lax.dot_general(pick, rows_ref[...], (((1,), (1,)), ((), ())), preferred_element_type=f32)
        one_ref[:, p * 512 : (p + 1) * 512] = edges[0:2]
        two_ref[:, p * 512 : (p + 1) * 512] = edges[2:4]


def y_edges(rows):
    shape = jax.ShapeDtypeStruct((2, 5 * 512), f32)
    return pl.pallas_call(
        edge_kernel,
        in_specs=[vmem],
        out_specs=[vmem, vmem],
        out_shape=[shape, shape],
        scratch_shapes=[pltpu.VMEM((512, 256), bf16)],
        cost_estimate=pl.CostEstimate(flops=0, bytes_accessed=ROWS * 512, transcendentals=0),
        compiler_params=pltpu.CompilerParams(vmem_limit_bytes=16 << 20),
        name="y_edges",
    )(rows)


def split(value):
    high = value.astype(bf16)
    low = (value - high.astype(f32)).astype(bf16)
    return high, low


def exact(pick, table):
    high, low = split(table)
    rest = (table - high.astype(f32) - low.astype(f32)).astype(bf16)
    total = jnp.dot(pick, high, preferred_element_type=f32)
    total = total + jnp.dot(pick, low, preferred_element_type=f32)
    return total + jnp.dot(pick, rest, preferred_element_type=f32)


def coupling(start, first, second, hermite):
    rows = 5 * PQ_PAD

    def row_ids(width):
        i = iota((rows, width), 0)
        c = jnp.zeros_like(i)
        for j in range(1, 5):
            c = c + (i >= PQ_PAD * j).astype(jnp.int32)
        ab = i - PQ_PAD * c
        a = tens(ab)
        return c, a + start, ab - 10 * a, ab < PQ

    def columns(height):
        k = iota((height, 128), 1)
        other = k >= K_HALF
        kk = jnp.where(other, k - K_HALF, k)
        p_here = tens(kk)
        p = p_here + jnp.where(other, 5 - start, start)
        return p, kk - 10 * p_here, kk < PQ

    p10, q10, ok10 = columns(10)
    source = iota((10, 128), 0)
    spread_p = one_hot(ok10 & (source == p10))
    spread_q = one_hot(ok10 & (source == q10))

    def table(flow, spread):
        return jnp.concatenate(
            [
                jnp.dot(flow, spread, precision=highest, preferred_element_type=f32),
                jnp.dot(hermite, spread, precision=highest, preferred_element_type=f32),
                jnp.zeros((6, 128), f32),
            ],
            axis=0,
        )

    c, a, b, valid = row_ids(56)
    t = iota((rows, 56), 1)
    pick_a = one_hot(valid & (t == jnp.where(c == 4, 40 + a, 4 * a + c))).astype(bf16)
    pick_b = one_hot(valid & (t == jnp.where(c == 4, 40 + b, 4 * b + c))).astype(bf16)
    left = exact(pick_a, table(first, spread_p))
    right = exact(pick_b, table(second, spread_q))
    c, a, b, _ = row_ids(128)
    p, q, _ = columns(rows)
    spring = c == 4
    both = left * jnp.where(spring, one_hot(b == q), right)
    both = both + jnp.where(spring & (a == p), right, 0.0)
    return time_step * both


def main_kernel(
    laguerre_ref,
    own_ref,
    other_ref,
    velocity_ref,
    shear_ref,
    first_ref,
    second_ref,
    hermite_ref,
    out_ref,
    data_ref,
    turned_ref,
    rate_ref,
    wide_ref,
    narrow_ref,
    coef_ref,
    mix_ref,
):
    matrix = coupling(5 * lax.axis_index("col"), first_ref[...], second_ref[...], hermite_ref[...])
    matrix_high, matrix_low = split(matrix)
    wide_ref[:, 0:128] = matrix_high
    wide_ref[:, 128:256] = matrix_high
    narrow_ref[...] = matrix_low

    u = velocity_ref[0:4, :]
    v = velocity_ref[4:8, :]
    lane = iota((4, 128), 1)
    u0, um1, um2, up1, up2 = upwind(u)
    v0, vm1, vm2, vp1, vp2 = upwind(v)
    coefs = (
        1.0 + u0 + v0,
        um1,
        um2,
        up1,
        up2,
        jnp.where(lane >= 1, vm1, 0.0),
        jnp.where(lane >= 2, vm2, 0.0),
        jnp.where(lane < 127, vp1, 0.0),
        jnp.where(lane < 126, vp2, 0.0),
    )
    for i, c in enumerate(coefs):
        coef_ref[i, 0:4, :] = c
    laguerre = time_step * laguerre_ref[...]
    for r in range(10):
        for s in range(10):
            mix_ref[10 * r + s] = jnp.broadcast_to(laguerre[r : r + 1, s : s + 1], (8, 128))

    def pack(rx, carry):
        base = pl.multiple_of((rx // 2) * 256, 256)
        lanes = pl.ds(pl.multiple_of(lax.rem(rx, 2) * 128, 128), 128)
        for i, ref in enumerate((own_ref, other_ref)):
            value = ref[pl.ds(rx, PQ, stride=RX), :]
            if i == 0:
                turned_ref[pl.ds(pl.multiple_of(rx * PQ_PAD, 8), PQ), :] = value
            high, low = split(value)
            for k, part in ((64 * i, high), (128 + 64 * i, low)):
                rows = pl.ds(base + k + 48, 16)
                data_ref[rows, lanes] = jnp.zeros((16, 128), bf16)
                data_ref[pl.ds(base + k, PQ), lanes] = part
        return carry

    lax.fori_loop(0, RX, pack, 0, unroll=PACK_UNROLL)

    def pair(i, carry):
        data = data_ref[pl.ds(pl.multiple_of(i * 256, 256), 256), :]
        product = jnp.dot(wide_ref[...], data, preferred_element_type=f32)
        product = product + jnp.dot(narrow_ref[...], data[0:128], preferred_element_type=f32)
        for t in range(2):
            rx = 2 * i + t
            x = lax.rem(rx, 4)
            part = product[:, t * 128 : (t + 1) * 128]
            total = part[4 * PQ_PAD : 5 * PQ_PAD]
            for c in range(4):
                total = total + shear_ref[pl.ds(4 * c + x, 1), :] * part[c * PQ_PAD : (c + 1) * PQ_PAD]
            rate_ref[pl.ds(pl.multiple_of(rx * PQ_PAD, 8), PQ_PAD), :] = total
        return carry

    lax.fori_loop(0, N_PAIR, pair, 0, unroll=PAIR_UNROLL)

    def strip(j, count):
        def field(r, x):
            return turned_ref[pl.ds(pl.multiple_of((4 * r + x) * PQ_PAD + 8 * j, 8), 8), :]

        def coef(i, x):
            return coef_ref[i, x : x + 1, :]

        for half in ((0, 1), (2, 3)):
            here = {x: [field(r, x) for r in range(10)] for x in half}
            for r in range(10):
                mix = [mix_ref[10 * r + s] for s in range(10)]
                for x in half:
                    f = here[x][r]
                    total = rate_ref[pl.ds(pl.multiple_of((4 * r + x) * PQ_PAD + 8 * j, 8), 8), :]
                    total = total + coef(0, x) * f
                    for s in range(10):
                        total = total + mix[s] * here[x][s]
                    for shift, i in ((-1, 1), (-2, 2), (1, 3), (2, 4)):
                        if 0 <= x + shift < 4:
                            total = total + coef(i, x) * field(r, x + shift)
                    for shift, i in ((1, 5), (2, 6), (127, 7), (126, 8)):
                        total = total + coef(i, x) * pltpu.roll(f, shift, 1)
                    out_ref[pl.ds(j * (8 * RX) + 4 * r + x, count, stride=RX), :] = total[0:count]

    def whole(j, carry):
        strip(j, 8)
        return carry

    lax.fori_loop(0, PQ // 8, whole, 0, unroll=STRIP_UNROLL)
    strip(PQ // 8, PQ % 8)


def main(laguerre, own, other, velocity, shear, first, second, hermite):
    return pl.pallas_call(
        main_kernel,
        in_specs=[vmem] * 8,
        out_specs=vmem,
        out_shape=jax.ShapeDtypeStruct((ROWS, 128), f32),
        scratch_shapes=[
            pltpu.VMEM((N_PAIR * 256, 256), bf16),
            pltpu.VMEM((PQ_PAD * RX, 128), f32),
            pltpu.VMEM((PQ_PAD * RX, 128), f32),
            pltpu.VMEM((5 * PQ_PAD, 256), bf16),
            pltpu.VMEM((5 * PQ_PAD, 128), bf16),
            pltpu.VMEM((9, 8, 128), f32),
            pltpu.VMEM((100, 8, 128), f32),
        ],
        compiler_params=pltpu.CompilerParams(vmem_limit_bytes=24 << 20),
        cost_estimate=pl.CostEstimate(flops=2 * 280 * 384 * 5120, bytes_accessed=3 * ROWS * 512, transcendentals=0),
        name="main_step",
    )(laguerre, own, other, velocity, shear, first, second, hermite)


def final_kernel(
    partial_ref,
    x_one_ref,
    x_two_ref,
    y_one_ref,
    y_two_ref,
    velocity_ref,
    weight_ref,
    out_hbm,
    stress_ref,
    out_ref,
    sems,
):
    odd_x = lax.rem(lax.axis_index("gx"), 2) == 0
    odd_y = lax.rem(lax.axis_index("gy"), 2) == 1

    def halo(on_left, p, k):
        layer = pl.ds(MODES_P * (2 * p + k), MODES_P)
        one, two = x_one_ref[layer, :], x_two_ref[layer, :]
        return jnp.where(odd_x, one, two) if on_left else jnp.where(odd_x, two, one)

    u = velocity_ref[0:4, :]
    v = velocity_ref[4:8, :]
    lane4 = iota((4, 128), 1)
    _, um1, um2, up1, up2 = upwind(u)
    _, vm1, vm2, vp1, vp2 = upwind(v)
    near = jnp.where(lane4 == 0, vm1, jnp.where(lane4 == 127, vp1, 0.0))
    far = jnp.where(lane4 <= 1, vm2, jnp.where(lane4 >= 126, vp2, 0.0))
    row = lax.rem(iota((32, 256), 0), 8)
    lane = iota((32, 256), 1)
    hit = (row == 1) & ((lane == 0) | (lane == 129))
    hit = hit | ((row == 2) & ((lane == 127) | (lane == 254)))
    hit = hit | ((row == 0) & (lane == 128))
    hit = hit | ((row == 3) & (lane == 255))
    place = one_hot(hit).astype(bf16)
    stress = [jnp.zeros((1, 128), f32) for _ in range(12)]
    copies = []
    for p in range(5):
        lanes = slice(p * 512, (p + 1) * 512)
        y_one = y_one_ref[:, lanes]
        y_two = y_two_ref[:, lanes]
        below = jnp.where(odd_y, y_one, y_two)
        above = jnp.where(odd_y, y_two, y_one)
        edges = jnp.concatenate([below, above, jnp.zeros((4, 512), f32)], axis=0)
        high = edges.astype(bf16).astype(f32)
        rest = edges - high
        middle = rest.astype(bf16).astype(f32)
        low = rest - middle
        stacked = jnp.concatenate([high, middle, low, jnp.zeros((8, 512), f32)], axis=0).astype(bf16)
        spread = lax.dot_general(stacked, place, (((0,), (0,)), ((), ())), preferred_element_type=f32)
        left_far = halo(True, p, 0)
        left_near = halo(True, p, 1)
        right_near = halo(False, p, 0)
        right_far = halo(False, p, 1)
        for x in range(4):
            total = partial_ref[pl.ds(400 * p + x, MODES_P, stride=4), :]
            total = total + near[x : x + 1] * spread[x * 128 : x * 128 + MODES_P, 0:128]
            total = total + far[x : x + 1] * spread[x * 128 : x * 128 + MODES_P, 128:256]
            if x == 0:
                total = total + um1[0:1] * left_near + um2[0:1] * left_far
            if x == 1:
                total = total + um2[1:2] * left_near
            if x == 2:
                total = total + up2[2:3] * right_near
            if x == 3:
                total = total + up1[3:4] * right_near + up2[3:4] * right_far
            out_ref[pl.ds(400 * p + x, MODES_P, stride=4), :] = total
            for s in range(3):
                moment = jnp.sum(weight_ref[p, :, s : s + 1] * total, axis=0, keepdims=True)
                stress[4 * s + x] = stress[4 * s + x] + moment
        rows = pl.ds(400 * p, 400)
        copies.append(pltpu.make_async_copy(out_ref.at[rows], out_hbm.at[rows], sems.at[p]))
        copies[-1].start()
    for s in range(3):
        for x in range(4):
            stress_ref[s, x : x + 1, :] = stress[4 * s + x]
    for copy in copies:
        copy.wait()


def final(partial, x_one, x_two, y_one, y_two, velocity, weights):
    return pl.pallas_call(
        final_kernel,
        in_specs=[vmem] * 7,
        out_specs=[hbm, vmem],
        out_shape=[jax.ShapeDtypeStruct((ROWS, 128), f32), jax.ShapeDtypeStruct((3, 4, 128), f32)],
        scratch_shapes=[pltpu.VMEM((ROWS, 128), f32), pltpu.SemaphoreType.DMA((5,))],
        cost_estimate=pl.CostEstimate(flops=20 * ROWS * 128, bytes_accessed=4 * ROWS * 512, transcendentals=0),
        compiler_params=pltpu.CompilerParams(vmem_limit_bytes=16 << 20),
        name="final_step",
    )(partial, x_one, x_two, y_one, y_two, velocity, weights)


def body(
    density,
    velocity,
    shear_rates,
    hermite_matrix,
    laguerre_matrix,
    flow_first,
    flow_second,
    stress_weights,
):
    rows = density.reshape(ROWS, 128)
    speeds = velocity.reshape(8, 128)
    shear = shear_rates.reshape(16, 128)
    first = jnp.transpose(flow_first, (1, 0, 2)).reshape(40, 10)
    second = jnp.transpose(flow_second, (1, 0, 2)).reshape(40, 10)
    weights = jnp.transpose(stress_weights.reshape(3, 5, MODES_P), (1, 2, 0))
    def pairings(axis, periodic):
        count = lax.axis_size(axis)
        one = [(i, i + 1) for i in range(0, count, 2)]
        two = [(i, (i + 1) % count) for i in range(1, count if periodic else count - 1, 2)]
        return [pairs + [(b, a) for a, b in pairs] for pairs in (one, two)]

    ring_two, ring_one = pairings("gx", True)
    line_one, line_two = pairings("gy", False)
    send_one, send_two = x_halos(rows)
    x_one = lax.ppermute(send_one, "gx", ring_one)
    x_two = lax.ppermute(send_two, "gx", ring_two)
    send_one, send_two = y_edges(rows)
    y_one = lax.ppermute(send_one, "gy", line_one)
    y_two = lax.ppermute(send_two, "gy", line_two)
    other = lax.ppermute(rows, "col", [(0, 1), (1, 0)])
    partial = main(laguerre_matrix, rows, other, speeds, shear, first, second, hermite_matrix)
    advanced, stress = final(partial, x_one, x_two, y_one, y_two, speeds, weights)
    stress = lax.psum(stress, "col")
    return (advanced.reshape(density.shape), stress)


def solution(mesh):
    in_specs = (
        P("col", None, None, "gx", "gy"),
        P(None, "gx", "gy"),
        P(None, "gx", "gy"),
        P(),
        P(),
        P(),
        P(),
        P(None, "col", None, None),
    )
    out_specs = (P("col", None, None, "gx", "gy"), P(None, "gx", "gy"))
    return jax.shard_map(body, mesh=mesh, in_specs=in_specs, out_specs=out_specs, check_vma=False)
```
